256 devices in a mesh: ka: 32 (over y, z_hi, x), occ: 8 (over z_lo, core).
Axes of the slice: x: 4, y: 4, z: 8 (z_hi: 2, z_lo: 4; z = z_hi * 4 + z_lo), core: 2. Of those that a mesh axis runs over, the one named last changes fastest.
Arguments:
- factors: bfloat16 [64, 8, 192, 2, 768], P('ka'), may hold values from -0.23925781 to 0.23925781
- occupied_energy: float32 [8], replicated, may hold values from -2 to -0.5
- virtual_energy: bfloat16 [64, 192], P('ka'), may hold values from 0.5 to 3
- conserve: int32 [64, 2], P('ka'), may hold values from 0 to 63, as said below
- pair_lists: int32 [2, 16, 2], P(None, 'occ'), may hold values from 0 to 7, as said below
Outputs:
- density: float32 [64, 192, 2, 192], P('ka', 'occ')
The draws below stay inside these ranges and needn't reach their ends.
Inputs may be any that keep to these rules, and one draw needn't show every extreme that they name: For a momentum ka among the 2 momenta of block d (momenta d * 2 to d * 2 + 1), (64 - conserve[ka, r]) mod 64 lies in block (d - r - 1) mod 32; the 2 momenta of one block name different momenta in each round. `pair_lists`: each entry is an ordered pair (i, j) of occupied orbitals; every round begins with the pairs (0, 0) and (7, 7); within a round no ordered pair repeats (16 of the 64 ordered pairs appear).
All inputs are finite; a program needn't handle non-finite values.
Results may differ from the reference program's by a relative error of at most 0.00082.
Values may be sent and summed in bfloat16 or wider, within the bound.
No kernel may reach another device: no remote copies, remote signals or barrier semaphores. Data moves between devices by JAX's collectives and lax.ppermute only.
A program may use at most 128 MiB of HBM per device.

```python
import jax
import jax.numpy as jnp
from jax import lax

NV = 192
NAUX = 768
KA_DEV = 2
ROUNDS = 2
NK = 64
NOCC = 8
NPAIRS = 16


def draw_conserve(key, part):
    groups = NK // KA_DEV
    row_keys = jax.random.split(jax.random.fold_in(key, 7), groups * ROUNDS)
    orders = jax.vmap(lambda single: jax.random.permutation(single, KA_DEV))(row_keys)
    orders = orders.reshape(groups, ROUNDS, KA_DEV).transpose(0, 2, 1).astype(jnp.int32)
    device = jnp.arange(groups, dtype=jnp.int32)[:, None, None]
    round_ids = jnp.arange(ROUNDS, dtype=jnp.int32)[None, None, :]
    source = (device - round_ids - 1) % groups
    mirror = source * KA_DEV + orders
    return ((NK - mirror) % NK).reshape(NK, ROUNDS).astype(jnp.int32)


def draw_pair_lists(key, part):
    square = NOCC * NOCC
    round_keys = jax.random.split(jax.random.fold_in(key, 11), ROUNDS)
    middle = jax.vmap(lambda single: jax.random.permutation(single, square - 2))(round_keys).astype(jnp.int32) + 1
    ends = jnp.broadcast_to(jnp.array([0, square - 1], dtype=jnp.int32)[None, :], (ROUNDS, 2))
    orders = jnp.concatenate([ends, middle], axis=1)
    positions = jnp.arange(NPAIRS, dtype=jnp.int32)
    picked = orders[:, positions % square]
    extra = jax.random.randint(jax.random.fold_in(key, 13), (ROUNDS, NPAIRS), 0, square).astype(jnp.int32)
    flat = jnp.where(positions[None, :] < square, picked, extra)
    leading = flat // NOCC
    trailing = flat % NOCC
    return jnp.stack([leading, trailing], axis=-1).astype(jnp.int32)


def block_levels(rng, dims, cuts, smallest, largest):
    def one(position, parts):
        steps = jax.random.uniform(jax.random.fold_in(jax.random.fold_in(rng, 6), position), (parts,), jnp.float32, smallest / len(cuts), largest / len(cuts))
        return jnp.repeat(jnp.exp(steps), dims[position] // parts).reshape((-1,) + (1,) * (len(dims) - position - 1))

    gain = one(*cuts[0])
    for cut in cuts[1:]:
        gain = gain * one(*cut)
    return gain


def normal_values(own_key, extent, spread, most, cuts=(), kind=jnp.bfloat16):
    entries = spread * jax.random.normal(own_key, extent, jnp.float32)
    if cuts:
        entries = entries * block_levels(own_key, extent, cuts, -0.22, 0.18)
    return jnp.clip(entries, -most, most).astype(kind)


def setup_inputs(seed: int = 0) -> dict:
    seeds = jax.random.split(jax.random.key(seed), 6)
    factors = normal_values(seeds[0], (NK, NOCC, NV, 2, NAUX), 0.04, 0.23925781, ((0, 32),))
    occupied_energy = jnp.clip(jax.random.uniform(seeds[1], (NOCC,), jnp.float32, -2.0, -0.5), -2.0, -0.5)
    virtual_energy = jnp.clip(0.5 + 2.5 * jax.random.uniform(seeds[2], (NK, NV), jnp.float32) ** block_levels(seeds[2], (NK, NV), ((0, 32),), -0.2, 0.2), 0.5, 3.0).astype(jnp.bfloat16)
    conserve = draw_conserve(jax.random.fold_in(seeds[5], 71), 0)
    pair_lists = draw_pair_lists(jax.random.fold_in(seeds[5], 71), 0)
    return {"factors": factors, "occupied_energy": occupied_energy, "virtual_energy": virtual_energy, "conserve": conserve, "pair_lists": pair_lists}


def build_mates(received, auxiliary):
    real_part = received[..., :auxiliary]
    imaginary = received[..., auxiliary:]
    turned = jnp.concatenate([-imaginary, real_part], axis=-1)
    return jnp.concatenate([received, turned], axis=-2)


def amplitude(left_rows, mate_rows, energy_left, energy_right, occupied_sum):
    values = lax.dot_general(left_rows, mate_rows, (((1,), (1,)), ((), ())), preferred_element_type=jnp.float32)
    denominator = energy_left[:, None] + energy_right[None, :] - occupied_sum
    return values / jnp.concatenate([denominator, denominator], axis=1)


def density_term(amplitudes, swapped):
    virtuals = amplitudes.shape[0]
    combined = (2.0 * amplitudes - swapped).astype(jnp.bfloat16)
    rounded = amplitudes.astype(jnp.bfloat16)
    turned = jnp.concatenate([-rounded[:, virtuals:], rounded[:, :virtuals]], axis=1)
    stacked = jnp.concatenate([rounded, turned], axis=0)
    return lax.dot_general(combined, stacked, (((1,), (1,)), ((), ())), preferred_element_type=jnp.float32)


def pair_term(own_block, mate_block, energy_left, energy_right, occupied_energy, pair_row):
    leading = pair_row[0]
    trailing = pair_row[1]
    occupied_sum = occupied_energy[leading] + occupied_energy[trailing]
    amplitudes = amplitude(own_block[leading], mate_block[trailing], energy_left, energy_right, occupied_sum)
    swapped = amplitude(own_block[trailing], mate_block[leading], energy_left, energy_right, occupied_sum)
    return density_term(amplitudes, swapped)


def reference(factors, occupied_energy, virtual_energy, conserve, pair_lists):
    momentum_count = factors.shape[0]
    orbitals = factors.shape[1]
    virtuals = factors.shape[2]
    auxiliary = factors.shape[4]
    stacked = factors.reshape(momentum_count, orbitals, virtuals, 2 * auxiliary)
    energies = virtual_energy.astype(jnp.float32)

    def one_momentum(moment):
        own_block = stacked[moment]
        energy_left = energies[moment]
        running = jnp.zeros((virtuals, 2 * virtuals), jnp.float32)
        for round_index in range(conserve.shape[1]):
            mirror = ((momentum_count - conserve[moment, round_index]) % momentum_count).astype(jnp.int32)
            mate_block = build_mates(stacked[mirror], auxiliary)
            energy_right = energies[mirror]

            def add_pair(partial_sum, pair_row):
                term = pair_term(own_block, mate_block, energy_left, energy_right, occupied_energy, pair_row)
                return partial_sum + term, None

            running, ignored = lax.scan(add_pair, running, pair_lists[round_index])
        return running.reshape(virtuals, 2, virtuals)

    return lax.map(one_momentum, jnp.arange(momentum_count, dtype=jnp.int32))
```

```python
import functools

import jax
import jax.numpy as jnp
from jax import lax
from jax.experimental import pallas as pl
from jax.experimental.pallas import tpu as pltpu
from jax.sharding import PartitionSpec as P

ROWS, COLUMNS, LINE, CORES = 8, 4, 4, 2


def device_index(row, column, place, core):
    return ((row % ROWS) * COLUMNS + column % COLUMNS) * LINE * CORES + place * CORES + core


def route(target):
    pairs = []
    for row in range(ROWS):
        for column in range(COLUMNS):
            for place in range(LINE):
                for core in range(CORES):
                    goal = target(row, column, place, core)
                    if goal is not None:
                        pairs.append((device_index(row, column, place, core), device_index(*goal)))
    return pairs


def shifted(by):
    def target(row, column, place, core):
        if column + by < COLUMNS:
            return row, column + by, place, core
        return row + 1, column + by - COLUMNS, LINE - 1 - place, core

    return route(target)


def round_kernel(first, chosen, pairs, place_ref, occupied, left_re, left_im, mate, own_energy, *refs):
    if first:
        keep, send, products, combined, rounded, turned, total = refs
    else:
        keep_in, send_in, keep, send, products, combined, rounded, turned, total = refs
    half = pl.program_id(0)
    step = pl.program_id(1)
    steps = pl.num_programs(1)
    per_step = left_re.shape[1]
    orbitals = steps_orbitals = products.shape[0]
    rows = products.shape[2]
    share = rows // (2 * orbitals)
    count = pairs.shape[0]
    virtuals = products.shape[3]
    piece = mate[0, :rows]
    contract = (((1,), (1,)), ((), ()))
    for inner in range(per_step):
        orbital = step * per_step + inner
        products[orbital, 0] = lax.dot_general(
            piece, left_re[0, inner], contract, preferred_element_type=jnp.float32
        )
        products[orbital, 1] = lax.dot_general(
            piece, left_im[0, inner], contract, preferred_element_type=jnp.float32
        )

    @pl.when(step == steps - 1)
    def _():
        energy_row = mate[0, rows : rows + 1, :128].astype(jnp.float32)
        spread = jnp.broadcast_to(energy_row, (share, 128))
        on_diagonal = lax.broadcasted_iota(jnp.int32, (share, 128), 0) == lax.broadcasted_iota(
            jnp.int32, (share, 128), 1
        )
        energy_mate = jnp.sum(jnp.where(on_diagonal, spread, 0.0), axis=1, keepdims=True)
        energy_sum = own_energy[0] + energy_mate

        def exchange(lead, trail):
            top = pl.multiple_of(trail * share, 8)
            bottom = pl.multiple_of((orbitals + trail) * share, 8)
            real = products[lead, 0, pl.ds(top, share)] + products[lead, 1, pl.ds(bottom, share)]
            imaginary = products[lead, 1, pl.ds(top, share)] - products[lead, 0, pl.ds(bottom, share)]
            return real, imaginary

        def one_pair(index):
            lead = pairs[index, 0]
            trail = pairs[index, 1]
            inverse = 1.0 / (energy_sum - (occupied[lead] + occupied[trail]))
            real, imaginary = exchange(lead, trail)
            swapped_real, swapped_imaginary = exchange(trail, lead)
            real, imaginary = real * inverse, imaginary * inverse
            return (
                2.0 * real - swapped_real * inverse,
                2.0 * imaginary - swapped_imaginary * inverse,
                real,
                imaginary,
            )

        def two_pairs(index, carry):
            low = one_pair(2 * index)
            high = one_pair(2 * index + 1)
            c_re, c_im, a_re, a_im = (
                jnp.concatenate([x, y], axis=0).astype(jnp.bfloat16) for x, y in zip(low, high)
            )
            top = pl.ds(pl.multiple_of(index * 2 * share, 16), 2 * share)
            bottom = pl.ds(pl.multiple_of((count + index * 2) * share, 16), 2 * share)
            combined[top] = c_re
            combined[bottom] = c_im
            rounded[top] = a_re
            rounded[bottom] = a_im
            turned[top] = -a_im
            turned[bottom] = a_re
            return carry

        lax.fori_loop(0, count // 2, two_pairs, 0)
        contract_rows = (((0,), (0,)), ((), ()))
        total[0] = lax.dot_general(
            combined[...], rounded[...], contract_rows, preferred_element_type=jnp.float32
        )
        total[1] = lax.dot_general(
            combined[...], turned[...], contract_rows, preferred_element_type=jnp.float32
        )
        mine = chosen[half]
        core = place_ref[0]
        for place in range(keep.shape[0]):
            for target, offset in ((keep, core), (send, 1 - core)):
                cut = pl.ds(pl.multiple_of((place * CORES + offset) * share, 8), share)
                value = total[:, cut]
                if not first:
                    value = value + (keep_in if target is keep else send_in)[place, mine]
                target[place, mine] = value


def round_density(chosen, pairs, core, occupied, left_re, left_im, mate, own_energy, before):
    momenta, orbitals, virtuals, auxiliary = left_re.shape
    share = virtuals // (LINE * CORES)
    per_step = 2
    count = pairs.shape[0]
    rows = 2 * orbitals * share
    block = jax.ShapeDtypeStruct((LINE, momenta, 2, share, virtuals), jnp.float32)
    whole = pl.BlockSpec((LINE, momenta, 2, share, virtuals), lambda m, s, *_: (0, 0, 0, 0, 0))
    left = pl.BlockSpec((1, per_step, virtuals, auxiliary), lambda m, s, chosen, *_: (chosen[m], s, 0, 0))
    in_specs = [
        pl.BlockSpec(memory_space=pltpu.SMEM),
        left,
        left,
        pl.BlockSpec((1, mate.shape[1], auxiliary), lambda m, s, *_: (m, 0, 0)),
        pl.BlockSpec((1, 1, virtuals), lambda m, s, chosen, *_: (chosen[m], 0, 0)),
    ]
    if before:
        in_specs += [whole, whole]
    return pl.pallas_call(
        functools.partial(round_kernel, not before),
        out_shape=(block, block),
        grid_spec=pltpu.PrefetchScalarGridSpec(
            num_scalar_prefetch=3,
            grid=(momenta, orbitals // per_step),
            in_specs=in_specs,
            out_specs=(whole, whole),
            scratch_shapes=[
                pltpu.VMEM((orbitals, 2, rows, virtuals), jnp.float32),
                pltpu.VMEM((2 * count * share, virtuals), jnp.bfloat16),
                pltpu.VMEM((2 * count * share, virtuals), jnp.bfloat16),
                pltpu.VMEM((2 * count * share, virtuals), jnp.bfloat16),
                pltpu.VMEM((2, virtuals, virtuals), jnp.float32),
            ],
        ),
        compiler_params=pltpu.CompilerParams(
            dimension_semantics=("arbitrary", "arbitrary"), vmem_limit_bytes=40 << 20
        ),
        cost_estimate=pl.CostEstimate(
            flops=momenta * (4 * rows * virtuals * auxiliary * orbitals + 8 * count * share * virtuals * virtuals),
            bytes_accessed=momenta * orbitals * virtuals * auxiliary * 4 + 2 * momenta * rows * auxiliary,
            transcendentals=0,
        ),
    )(chosen, pairs, core, occupied, left_re, left_im, mate, own_energy, *before)


def summed(keep, send):
    place = lax.axis_index("occ") // CORES
    devices = LINE * CORES
    held = keep + lax.ppermute(send, "occ", [(i, i ^ 1) for i in range(devices)])
    total = lax.dynamic_index_in_dim(held, place, 0, keepdims=False)
    for hop in range(1, LINE):
        part = lax.dynamic_index_in_dim(held, (place + hop) % LINE, 0, keepdims=False)
        ring = [(i, (i + CORES * hop) % devices) for i in range(devices)]
        total = total + lax.ppermute(part, "occ", ring)
    return jnp.transpose(total, (0, 2, 1, 3))


def local(factors, occupied_energy, virtual_energy, conserve, pair_lists):
    momenta, orbitals, virtuals, _, auxiliary = factors.shape
    devices = lax.axis_size("occ")
    share = virtuals // devices
    start = lax.axis_index("occ") * share
    cut = lax.dynamic_slice_in_dim(factors, start, share, 2)
    cut = jnp.transpose(cut, (0, 3, 1, 2, 4)).reshape(momenta, 2 * orbitals * share, auxiliary)
    energy_cut = lax.dynamic_slice_in_dim(virtual_energy, start, share, 1)
    energy_rows = jnp.pad(energy_cut[:, None, :], ((0, 0), (0, 7), (0, auxiliary - share)))
    outgoing = jnp.concatenate([cut, energy_rows], axis=1)
    left_re = factors[:, :, :, 0, :]
    left_im = factors[:, :, :, 1, :]
    own_energy = virtual_energy.astype(jnp.float32)[:, None, :]
    all_pairs = lax.all_gather(pair_lists, "occ", axis=1, tiled=True)
    core = (lax.axis_index("occ") % CORES).astype(jnp.int32).reshape(1)
    density = ()
    for round_index in range(conserve.shape[1]):
        mate = lax.ppermute(outgoing, ("ka", "occ"), shifted(round_index + 1))
        chosen = (conserve[0, round_index] + jnp.arange(momenta, dtype=jnp.int32)) % momenta
        density = round_density(
            chosen, all_pairs[round_index], core, occupied_energy, left_re, left_im, mate, own_energy, density
        )
    return summed(*density)


def solution(mesh):
    in_specs = (
        P("ka", None, None, None, None),
        P(),
        P("ka", None),
        P("ka", None),
        P(None, "occ", None),
    )
    out_specs = P("ka", "occ", None, None)
    return jax.shard_map(local, mesh=mesh, in_specs=in_specs, out_specs=out_specs, check_vma=False)
```

```python
import functools

import jax
import jax.numpy as jnp
from jax import lax
from jax.experimental import pallas as pl
from jax.experimental.pallas import tpu as pltpu
from jax.sharding import PartitionSpec as P

ROWS, COLUMNS, LINE, CORES = 8, 4, 4, 2
LANES, HEAD = 128, 8


def device_index(row, column, place, core):
    return ((row % ROWS) * COLUMNS + column) * LINE * CORES + place * CORES + core


def route(columns, by):
    pairs = []
    for row in range(ROWS):
        for column in columns:
            for place in range(LINE):
                for core in range(CORES):
                    goal = column + by
                    crosses = (column, by) in CROSSING
                    pairs.append(
                        (
                            device_index(row, column, place, core),
                            device_index(
                                row + crosses, goal % COLUMNS, LINE - 1 - place if crosses else place, core
                            ),
                        )
                    )
    return pairs


CROSSING = {(3, 1), (2, 2), (3, 2), (0, 0), (1, -1), (2, -1)}


def moved(array, columns, by):
    return lax.ppermute(array, ("ka", "occ"), route(columns, by))


def piece_kernel(later, chosen, pairs, flags, occupied, left, own_energy, *refs):
    mates = refs[:2]
    refs = refs[2:]
    if later:
        before, refs = refs[:4], refs[4:]
    keep, send, piece, products, combined, rounded, turned, total = refs
    orbitals = products.shape[0]
    virtuals = products.shape[3]
    rows = products.shape[2]
    share = rows // (2 * orbitals)
    count = pairs.shape[0]
    mine = chosen[0]
    first = flags[0] == 0

    @pl.when(first)
    def _():
        piece[...] = mates[0][...]

    @pl.when(jnp.logical_not(first))
    def _():
        piece[...] = mates[1][...]

    contract = (((1,), (1,)), ((), ()))
    for orbital in range(orbitals):
        for part in range(2):
            products[orbital, part] = lax.dot_general(
                piece[:rows],
                left[mine, orbital, part * virtuals : (part + 1) * virtuals],
                contract,
                preferred_element_type=jnp.float32,
            )

    energy_row = piece[rows : rows + 1, :LANES].astype(jnp.float32)
    spread = jnp.broadcast_to(energy_row, (share, LANES))
    on_diagonal = lax.broadcasted_iota(jnp.int32, (share, LANES), 0) == lax.broadcasted_iota(
        jnp.int32, (share, LANES), 1
    )
    energy_mate = jnp.sum(jnp.where(on_diagonal, spread, 0.0), axis=1, keepdims=True)
    energy_sum = own_energy[mine] + energy_mate

    def exchange(lead, trail):
        top = pl.ds(pl.multiple_of(trail * share, 8), share)
        bottom = pl.ds(pl.multiple_of((orbitals + trail) * share, 8), share)
        real = products[lead, 0, top] + products[lead, 1, bottom]
        imaginary = products[lead, 1, top] - products[lead, 0, bottom]
        return real, imaginary

    def one_pair(index):
        lead = pairs[index, 0]
        trail = pairs[index, 1]
        inverse = 1.0 / (energy_sum - (occupied[lead] + occupied[trail]))
        real, imaginary = exchange(lead, trail)
        swapped_real, swapped_imaginary = exchange(trail, lead)
        real, imaginary = real * inverse, imaginary * inverse
        return (
            2.0 * real - swapped_real * inverse,
            2.0 * imaginary - swapped_imaginary * inverse,
            real,
            imaginary,
        )

    def two_pairs(index, carry):
        low = one_pair(2 * index)
        high = one_pair(2 * index + 1)
        c_re, c_im, a_re, a_im = (
            jnp.concatenate([x, y], axis=0).astype(jnp.bfloat16) for x, y in zip(low, high)
        )
        top = pl.ds(pl.multiple_of(index * 2 * share, 16), 2 * share)
        bottom = pl.ds(pl.multiple_of((count + index * 2) * share, 16), 2 * share)
        combined[top] = c_re
        combined[bottom] = c_im
        rounded[top] = a_re
        rounded[bottom] = a_im
        turned[top] = -a_im
        turned[bottom] = a_re
        return carry

    lax.fori_loop(0, count // 2, two_pairs, 0)
    contract_rows = (((0,), (0,)), ((), ()))
    for part, right in enumerate((rounded, turned)):
        total[part] = lax.dot_general(
            combined[...], right[...], contract_rows, preferred_element_type=jnp.float32
        )
    core = flags[1]
    if later:
        same = flags[2] == 0
    for place in range(LINE):
        for out, target, offset in ((0, keep, core), (1, send, 1 - core)):
            cut = pl.ds(pl.multiple_of((place * CORES + offset) * share, 8), share)
            value = total[:, cut]
            if later:
                value = value + jnp.where(same, before[out][place], before[2 + out][place])
            target[place] = value


def piece_density(chosen, pairs, flags, occupied, left, own_energy, mates, before):
    orbitals, both, auxiliary = left.shape[1:]
    virtuals = both // 2
    share = virtuals // (LINE * CORES)
    count = pairs.shape[0]
    rows = 2 * orbitals * share
    block = jax.ShapeDtypeStruct((LINE, 2, share, virtuals), jnp.float32)
    scalars = pl.BlockSpec(memory_space=pltpu.SMEM)
    whole = pl.BlockSpec(memory_space=pltpu.VMEM)
    return pl.pallas_call(
        functools.partial(piece_kernel, bool(before)),
        out_shape=(block, block),
        in_specs=[scalars] * 4 + [whole] * (4 + len(before)),
        out_specs=(whole, whole),
        scratch_shapes=[
            pltpu.VMEM((rows + HEAD, auxiliary), jnp.bfloat16),
            pltpu.VMEM((orbitals, 2, rows, virtuals), jnp.float32),
            pltpu.VMEM((2 * count * share, virtuals), jnp.bfloat16),
            pltpu.VMEM((2 * count * share, virtuals), jnp.bfloat16),
            pltpu.VMEM((2 * count * share, virtuals), jnp.bfloat16),
            pltpu.VMEM((2, virtuals, virtuals), jnp.float32),
        ],
        compiler_params=pltpu.CompilerParams(vmem_limit_bytes=40 << 20),
        cost_estimate=pl.CostEstimate(
            flops=4 * rows * virtuals * auxiliary * orbitals + 8 * count * share * virtuals * virtuals,
            bytes_accessed=orbitals * both * auxiliary * 2 + 2 * rows * auxiliary,
            transcendentals=0,
        ),
    )(chosen, pairs, flags, occupied, left, own_energy, *mates, *before)


def summed(keep, send):
    place = lax.axis_index("occ") // CORES
    devices = LINE * CORES
    held = keep + lax.ppermute(send, "occ", [(i, i ^ 1) for i in range(devices)])
    total = lax.dynamic_index_in_dim(held, place, 0, keepdims=False)
    for hop in range(1, LINE):
        part = lax.dynamic_index_in_dim(held, (place + hop) % LINE, 0, keepdims=False)
        ring = [(i, (i + CORES * hop) % devices) for i in range(devices)]
        total = total + lax.ppermute(part, "occ", ring)
    return total


def all_pairs_of(pair_lists):
    gathered = pair_lists
    reach = 1
    while reach < LINE * CORES:
        other = lax.ppermute(gathered, "occ", [(i, i ^ reach) for i in range(LINE * CORES)])
        gathered = jnp.concatenate([gathered, other], axis=1)
        reach *= 2
    return gathered


def local(factors, occupied_energy, virtual_energy, conserve, pair_lists):
    momenta, orbitals, virtuals, _, auxiliary = factors.shape
    share = virtuals // (LINE * CORES)
    start = lax.axis_index("occ") * share

    def outgoing(momentum):
        cut = lax.dynamic_slice_in_dim(factors[momentum], start, share, 1)
        cut = jnp.transpose(cut, (2, 0, 1, 3)).reshape(2 * orbitals * share, auxiliary)
        energy = lax.dynamic_slice_in_dim(virtual_energy[momentum], start, share, 0)
        head = jnp.pad(energy[None, :], ((0, HEAD - 1), (0, auxiliary - share)))
        return jnp.concatenate([cut, head], axis=0)

    straight = outgoing(0)
    relayed = outgoing(1)
    cross_one = moved(straight, (3,), 1)
    cross_two = moved(straight, (2, 3), 2)
    hop_plus = lax.ppermute(relayed, ("ka", "occ"), ring_route(1))
    hop_minus = lax.ppermute(relayed, ("ka", "occ"), ring_route(-1))
    straight, hop_plus, hop_minus = lax.optimization_barrier((straight, hop_plus, hop_minus))
    up = moved(hop_plus, (0,), 0)
    back = moved(hop_minus, range(COLUMNS), -1)
    near_one = moved(straight, (0, 1, 2), 1)
    near_two = moved(straight, (0, 1), 2)

    left = jnp.transpose(factors, (0, 1, 3, 2, 4)).reshape(momenta, orbitals, 2 * virtuals, auxiliary)
    own_energy = virtual_energy.astype(jnp.float32)[:, None, :]
    pairs = all_pairs_of(pair_lists)
    core = lax.axis_index("occ") % CORES
    column = lax.axis_index("ka") % COLUMNS
    chosen = (conserve[0][:, None] + jnp.arange(momenta, dtype=jnp.int32)[None, :]) % momenta

    def density(round_index, momentum, mates, from_second, before, swapped):
        flags = jnp.stack([from_second.astype(jnp.int32), core.astype(jnp.int32), swapped])
        return piece_density(
            chosen[round_index, momentum].reshape(1), pairs[round_index], flags,
            occupied_energy, left, own_energy, mates, before,
        )

    zero = jnp.int32(0)
    early_b = density(0, 1, (up, hop_plus), column != 0, (), zero)
    early_a = density(0, 0, (cross_one, near_one), column != 0, (), zero)
    before = (*early_a, *early_b)
    late_b = density(1, 1, (back, back), column != column, before, (chosen[0, 0] != chosen[1, 1]).astype(jnp.int32))
    late_a = density(1, 0, (cross_two, near_two), column > 1, before, (chosen[0, 0] != chosen[1, 0]).astype(jnp.int32))
    of_b = summed(*late_b)
    of_a = summed(*late_a)
    stacked = jnp.stack([of_a, of_b])
    result = jnp.where(chosen[1, 0] == 0, stacked, stacked[::-1])
    return jnp.transpose(result, (0, 2, 1, 3))


def ring_route(by):
    pairs = []
    for row in range(ROWS):
        for column in range(COLUMNS):
            for place in range(LINE):
                for core in range(CORES):
                    pairs.append(
                        (
                            device_index(row, column, place, core),
                            device_index(row, (column + by) % COLUMNS, place, core),
                        )
                    )
    return pairs


def solution(mesh):
    in_specs = (
        P("ka", None, None, None, None),
        P(),
        P("ka", None),
        P("ka", None),
        P(None, "occ", None),
    )
    out_specs = P("ka", "occ", None, None)
    return jax.shard_map(local, mesh=mesh, in_specs=in_specs, out_specs=out_specs, check_vma=False)
```

```python
import functools

import jax
import jax.numpy as jnp
from jax import lax
from jax.experimental import pallas as pl
from jax.experimental.pallas import tpu as pltpu
from jax.sharding import PartitionSpec as P

ROWS, COLUMNS, LINE, CORES = 8, 4, 4, 2
LANES, HEAD = 128, 8


def device_index(row, column, place, core):
    return ((row % ROWS) * COLUMNS + column) * LINE * CORES + place * CORES + core


def route(columns, by):
    pairs = []
    for row in range(ROWS):
        for column in columns:
            for place in range(LINE):
                for core in range(CORES):
                    goal = column + by
                    crosses = (column, by) in CROSSING
                    pairs.append(
                        (
                            device_index(row, column, place, core),
                            device_index(
                                row + crosses, goal % COLUMNS, LINE - 1 - place if crosses else place, core
                            ),
                        )
                    )
    return pairs


CROSSING = {(3, 1), (2, 2), (3, 2), (0, 0), (1, -1), (2, -1)}


def moved(array, columns, by):
    return lax.ppermute(array, ("ka", "occ"), route(columns, by))


def piece_kernel(sources, later, chosen, pairs, flags, occupied, left, own_energy, *refs):
    mates, refs = refs[:sources], refs[sources:]
    if later:
        before, refs = refs[:4], refs[4:]
    keep, send, piece, products, combined, rounded, turned, total = refs
    orbitals = products.shape[0]
    virtuals = products.shape[3]
    rows = products.shape[2]
    share = rows // (2 * orbitals)
    count = pairs.shape[0]
    mine = chosen[0]
    for number, mate in enumerate(mates):

        @pl.when(flags[0] == number)
        def _():
            piece[...] = mate[...]

    contract = (((1,), (1,)), ((), ()))
    for orbital in range(orbitals):
        for part in range(2):
            products[orbital, part] = lax.dot_general(
                piece[:rows],
                left[mine, orbital, part * virtuals : (part + 1) * virtuals],
                contract,
                preferred_element_type=jnp.float32,
            )

    energy_row = piece[rows : rows + 1, :LANES].astype(jnp.float32)
    spread = jnp.broadcast_to(energy_row, (share, LANES))
    on_diagonal = lax.broadcasted_iota(jnp.int32, (share, LANES), 0) == lax.broadcasted_iota(
        jnp.int32, (share, LANES), 1
    )
    energy_mate = jnp.sum(jnp.where(on_diagonal, spread, 0.0), axis=1, keepdims=True)
    energy_sum = own_energy[mine] + energy_mate

    def exchange(lead, trail):
        top = pl.ds(pl.multiple_of(trail * share, 8), share)
        bottom = pl.ds(pl.multiple_of((orbitals + trail) * share, 8), share)
        real = products[lead, 0, top] + products[lead, 1, bottom]
        imaginary = products[lead, 1, top] - products[lead, 0, bottom]
        return real, imaginary

    def one_pair(index):
        lead = pairs[index, 0]
        trail = pairs[index, 1]
        inverse = 1.0 / (energy_sum - (occupied[lead] + occupied[trail]))
        real, imaginary = exchange(lead, trail)
        swapped_real, swapped_imaginary = exchange(trail, lead)
        real, imaginary = real * inverse, imaginary * inverse
        return (
            2.0 * real - swapped_real * inverse,
            2.0 * imaginary - swapped_imaginary * inverse,
            real,
            imaginary,
        )

    def two_pairs(index, carry):
        low = one_pair(2 * index)
        high = one_pair(2 * index + 1)
        c_re, c_im, a_re, a_im = (
            jnp.concatenate([x, y], axis=0).astype(jnp.bfloat16) for x, y in zip(low, high)
        )
        top = pl.ds(pl.multiple_of(index * 2 * share, 16), 2 * share)
        bottom = pl.ds(pl.multiple_of((count + index * 2) * share, 16), 2 * share)
        combined[top] = c_re
        combined[bottom] = c_im
        rounded[top] = a_re
        rounded[bottom] = a_im
        turned[top] = -a_im
        turned[bottom] = a_re
        return carry

    lax.fori_loop(0, count // 2, two_pairs, 0)
    contract_rows = (((0,), (0,)), ((), ()))
    for part, right in enumerate((rounded, turned)):
        total[part] = lax.dot_general(
            combined[...], right[...], contract_rows, preferred_element_type=jnp.float32
        )
    core = flags[1]
    if later:
        same = flags[2] == 0
    for place in range(LINE):
        for out, target, offset in ((0, keep, core), (1, send, 1 - core)):
            cut = pl.ds(pl.multiple_of((place * CORES + offset) * share, 8), share)
            value = total[:, cut]
            if later:
                value = value + jnp.where(same, before[out][place], before[2 + out][place])
            target[place] = value


def piece_density(chosen, pairs, flags, occupied, left, own_energy, mates, before):
    orbitals, both, auxiliary = left.shape[1:]
    virtuals = both // 2
    share = virtuals // (LINE * CORES)
    count = pairs.shape[0]
    rows = 2 * orbitals * share
    block = jax.ShapeDtypeStruct((LINE, 2, share, virtuals), jnp.float32)
    scalars = pl.BlockSpec(memory_space=pltpu.SMEM)
    whole = pl.BlockSpec(memory_space=pltpu.VMEM)
    return pl.pallas_call(
        functools.partial(piece_kernel, len(mates), bool(before)),
        out_shape=(block, block),
        in_specs=[scalars] * 4 + [whole] * (2 + len(mates) + len(before)),
        out_specs=(whole, whole),
        scratch_shapes=[
            pltpu.VMEM((rows + HEAD, auxiliary), jnp.bfloat16),
            pltpu.VMEM((orbitals, 2, rows, virtuals), jnp.float32),
            pltpu.VMEM((2 * count * share, virtuals), jnp.bfloat16),
            pltpu.VMEM((2 * count * share, virtuals), jnp.bfloat16),
            pltpu.VMEM((2 * count * share, virtuals), jnp.bfloat16),
            pltpu.VMEM((2, virtuals, virtuals), jnp.float32),
        ],
        compiler_params=pltpu.CompilerParams(vmem_limit_bytes=40 << 20),
        cost_estimate=pl.CostEstimate(
            flops=4 * rows * virtuals * auxiliary * orbitals + 8 * count * share * virtuals * virtuals,
            bytes_accessed=orbitals * both * auxiliary * 2 + 2 * rows * auxiliary,
            transcendentals=0,
        ),
    )(chosen, pairs, flags, occupied, left, own_energy, *mates, *before)


def summed(keep, send):
    place = lax.axis_index("occ") // CORES
    devices = LINE * CORES
    held = keep + lax.ppermute(send, "occ", [(i, i ^ 1) for i in range(devices)])
    total = lax.dynamic_index_in_dim(held, place, 0, keepdims=False)
    for hop in range(1, LINE):
        part = lax.dynamic_index_in_dim(held, (place + hop) % LINE, 0, keepdims=False)
        ring = [(i, (i + CORES * hop) % devices) for i in range(devices)]
        total = total + lax.ppermute(part, "occ", ring)
    return total


def all_pairs_of(pair_lists):
    gathered = pair_lists
    reach = 1
    while reach < LINE * CORES:
        other = lax.ppermute(gathered, "occ", [(i, i ^ reach) for i in range(LINE * CORES)])
        gathered = jnp.concatenate([gathered, other], axis=1)
        reach *= 2
    return gathered


def local(factors, occupied_energy, virtual_energy, conserve, pair_lists):
    momenta, orbitals, virtuals, _, auxiliary = factors.shape
    share = virtuals // (LINE * CORES)
    start = lax.axis_index("occ") * share

    def outgoing(momentum):
        cut = lax.dynamic_slice(
            factors, (momentum, 0, start, 0, 0), (1, orbitals, share, 2, auxiliary)
        )
        cut = jnp.transpose(cut[0], (2, 0, 1, 3)).reshape(2 * orbitals * share, auxiliary)
        energy = lax.dynamic_slice(virtual_energy, (momentum, start), (1, share))
        head = jnp.pad(energy, ((0, HEAD - 1), (0, auxiliary - share)))
        return jnp.concatenate([cut, head], axis=0)

    pairs = all_pairs_of(pair_lists)
    straight = outgoing(0)
    relayed = outgoing(1)
    straight, relayed, pairs, factors = lax.optimization_barrier((straight, relayed, pairs, factors))
    cross_one = moved(straight, (3,), 1)
    cross_two = moved(straight, (2,), 2)
    hop_plus = lax.ppermute(relayed, ("ka", "occ"), ring_route(1))
    hop_minus = lax.ppermute(relayed, ("ka", "occ"), ring_route(-1))
    left = jnp.transpose(factors, (0, 1, 3, 2, 4)).reshape(momenta, orbitals, 2 * virtuals, auxiliary)
    straight, hop_plus, hop_minus = lax.optimization_barrier((straight, hop_plus, hop_minus))
    up = moved(hop_plus, (0,), 0)
    back = moved(hop_minus, range(COLUMNS), -1)
    near_one = moved(straight, (0, 1, 2), 1)
    straight, cross_one, cross_two, near_one = lax.optimization_barrier((straight, cross_one, cross_two, near_one))
    late_two = moved(straight, (3,), 2)
    near_two = moved(straight, (0, 1), 2)

    own_energy = virtual_energy.astype(jnp.float32)[:, None, :]
    core = lax.axis_index("occ") % CORES
    column = lax.axis_index("ka") % COLUMNS
    chosen = (conserve[0][:, None] + jnp.arange(momenta, dtype=jnp.int32)[None, :]) % momenta

    def density(round_index, momentum, mates, source, before, swapped):
        flags = jnp.stack([source.astype(jnp.int32), core.astype(jnp.int32), swapped])
        return piece_density(
            chosen[round_index, momentum].reshape(1), pairs[round_index], flags,
            occupied_energy, left, own_energy, mates, before,
        )

    zero = jnp.int32(0)
    early_a = density(0, 0, (cross_one, near_one), column != 0, (), zero)
    early_b = density(0, 1, (up, hop_plus), column != 0, (), zero)
    before = (*early_a, *early_b)
    late_b = density(1, 1, (back,), zero, before, (chosen[0, 0] != chosen[1, 1]).astype(jnp.int32))
    source = jnp.clip(column, 0, 2)
    late_a = density(
        1, 0, (cross_two, late_two, near_two), source, before, (chosen[0, 0] != chosen[1, 0]).astype(jnp.int32)
    )
    of_b = summed(*late_b)
    of_a = summed(*late_a)
    stacked = jnp.stack([of_a, of_b])
    result = jnp.where(chosen[1, 0] == 0, stacked, stacked[::-1])
    return jnp.transpose(result, (0, 2, 1, 3))


def ring_route(by):
    pairs = []
    for row in range(ROWS):
        for column in range(COLUMNS):
            for place in range(LINE):
                for core in range(CORES):
                    pairs.append(
                        (
                            device_index(row, column, place, core),
                            device_index(row, (column + by) % COLUMNS, place, core),
                        )
                    )
    return pairs


def solution(mesh):
    in_specs = (
        P("ka", None, None, None, None),
        P(),
        P("ka", None),
        P("ka", None),
        P(None, "occ", None),
    )
    out_specs = P("ka", "occ", None, None)
    return jax.shard_map(local, mesh=mesh, in_specs=in_specs, out_specs=out_specs, check_vma=False)
```

```python
import functools

import jax
import jax.numpy as jnp
from jax import lax
from jax.experimental import pallas as pl
from jax.experimental.pallas import tpu as pltpu
from jax.sharding import PartitionSpec as P

ROWS, COLUMNS, LINE, CORES = 8, 4, 4, 2
LANES, HEAD = 128, 8


def device_index(row, column, place, core):
    return ((row % ROWS) * COLUMNS + column) * LINE * CORES + place * CORES + core


def route(columns, by):
    pairs = []
    for row in range(ROWS):
        for column in columns:
            for place in range(LINE):
                for core in range(CORES):
                    goal = column + by
                    crosses = (column, by) in CROSSING
                    pairs.append(
                        (
                            device_index(row, column, place, core),
                            device_index(
                                row + crosses, goal % COLUMNS, LINE - 1 - place if crosses else place, core
                            ),
                        )
                    )
    return pairs


CROSSING = {(3, 1), (2, 2), (3, 2), (0, 0), (1, -1), (2, -1)}


def moved(array, columns, by):
    return lax.ppermute(array, ("ka", "occ"), route(columns, by))


def piece_kernel(sources, later, chosen, pairs, flags, occupied, left, own_energy, *refs):
    mates, refs = refs[:sources], refs[sources:]
    if later:
        before, refs = refs[:4], refs[4:]
    keep, send, piece, products, combined, rounded, turned, total = refs
    orbitals = products.shape[0]
    virtuals = products.shape[3]
    rows = products.shape[2]
    share = rows // (2 * orbitals)
    count = pairs.shape[0]
    mine = chosen[0]
    for number, mate in enumerate(mates):

        @pl.when(flags[0] == number)
        def _():
            piece[...] = mate[...]

    contract = (((1,), (1,)), ((), ()))
    for orbital in range(orbitals):
        for part in range(2):
            products[orbital, part] = lax.dot_general(
                piece[:rows],
                left[mine, orbital, part * virtuals : (part + 1) * virtuals],
                contract,
                preferred_element_type=jnp.float32,
            )

    energy_row = piece[rows : rows + 1, :LANES].astype(jnp.float32)
    spread = jnp.broadcast_to(energy_row, (share, LANES))
    on_diagonal = lax.broadcasted_iota(jnp.int32, (share, LANES), 0) == lax.broadcasted_iota(
        jnp.int32, (share, LANES), 1
    )
    energy_mate = jnp.sum(jnp.where(on_diagonal, spread, 0.0), axis=1, keepdims=True)
    energy_sum = own_energy[mine] + energy_mate

    def exchange(lead, trail):
        top = pl.ds(pl.multiple_of(trail * share, 8), share)
        bottom = pl.ds(pl.multiple_of((orbitals + trail) * share, 8), share)
        real = products[lead, 0, top] + products[lead, 1, bottom]
        imaginary = products[lead, 1, top] - products[lead, 0, bottom]
        return real, imaginary

    def one_pair(index):
        lead = pairs[index, 0]
        trail = pairs[index, 1]
        inverse = 1.0 / (energy_sum - (occupied[lead] + occupied[trail]))
        real, imaginary = exchange(lead, trail)
        swapped_real, swapped_imaginary = exchange(trail, lead)
        real, imaginary = real * inverse, imaginary * inverse
        return (
            2.0 * real - swapped_real * inverse,
            2.0 * imaginary - swapped_imaginary * inverse,
            real,
            imaginary,
        )

    def two_pairs(index, carry):
        low = one_pair(2 * index)
        high = one_pair(2 * index + 1)
        c_re, c_im, a_re, a_im = (
            jnp.concatenate([x, y], axis=0).astype(jnp.bfloat16) for x, y in zip(low, high)
        )
        top = pl.ds(pl.multiple_of(index * 2 * share, 16), 2 * share)
        bottom = pl.ds(pl.multiple_of((count + index * 2) * share, 16), 2 * share)
        combined[top] = c_re
        combined[bottom] = c_im
        rounded[top] = a_re
        rounded[bottom] = a_im
        turned[top] = -a_im
        turned[bottom] = a_re
        return carry

    lax.fori_loop(0, count // 2, two_pairs, 0)
    contract_rows = (((0,), (0,)), ((), ()))
    for part, right in enumerate((rounded, turned)):
        total[part] = lax.dot_general(
            combined[...], right[...], contract_rows, preferred_element_type=jnp.float32
        )
    core = flags[1]
    if later:
        same = flags[2] == 0
    for place in range(LINE):
        for out, target, offset in ((0, keep, core), (1, send, 1 - core)):
            cut = pl.ds(pl.multiple_of((place * CORES + offset) * share, 8), share)
            value = total[:, cut]
            if later:
                value = value + jnp.where(same, before[out][place], before[2 + out][place])
            target[place] = value


def piece_density(chosen, pairs, flags, occupied, left, own_energy, mates, before):
    orbitals, both, auxiliary = left.shape[1:]
    virtuals = both // 2
    share = virtuals // (LINE * CORES)
    count = pairs.shape[0]
    rows = 2 * orbitals * share
    block = jax.ShapeDtypeStruct((LINE, 2, share, virtuals), jnp.float32)
    scalars = pl.BlockSpec(memory_space=pltpu.SMEM)
    whole = pl.BlockSpec(memory_space=pltpu.VMEM)
    return pl.pallas_call(
        functools.partial(piece_kernel, len(mates), bool(before)),
        out_shape=(block, block),
        in_specs=[scalars] * 4 + [whole] * (2 + len(mates) + len(before)),
        out_specs=(whole, whole),
        scratch_shapes=[
            pltpu.VMEM((rows + HEAD, auxiliary), jnp.bfloat16),
            pltpu.VMEM((orbitals, 2, rows, virtuals), jnp.float32),
            pltpu.VMEM((2 * count * share, virtuals), jnp.bfloat16),
            pltpu.VMEM((2 * count * share, virtuals), jnp.bfloat16),
            pltpu.VMEM((2 * count * share, virtuals), jnp.bfloat16),
            pltpu.VMEM((2, virtuals, virtuals), jnp.float32),
        ],
        compiler_params=pltpu.CompilerParams(vmem_limit_bytes=40 << 20),
        cost_estimate=pl.CostEstimate(
            flops=4 * rows * virtuals * auxiliary * orbitals + 8 * count * share * virtuals * virtuals,
            bytes_accessed=orbitals * both * auxiliary * 2 + 2 * rows * auxiliary,
            transcendentals=0,
        ),
    )(chosen, pairs, flags, occupied, left, own_energy, *mates, *before)


def summed(keep, send):
    place = lax.axis_index("occ") // CORES
    devices = LINE * CORES
    held = keep + lax.ppermute(send, "occ", [(i, i ^ 1) for i in range(devices)])
    total = lax.dynamic_index_in_dim(held, place, 0, keepdims=False)
    for hop in range(1, LINE):
        part = lax.dynamic_index_in_dim(held, (place + hop) % LINE, 0, keepdims=False)
        ring = [(i, (i + CORES * hop) % devices) for i in range(devices)]
        total = total + lax.ppermute(part, "occ", ring)
    return total


def line_pairs_of(pair_lists):
    parts = [pair_lists]
    for reach in range(1, LINE):
        swap = [(i, i ^ (CORES * reach)) for i in range(LINE * CORES)]
        parts.append(lax.ppermute(pair_lists, "occ", swap))
    return jnp.concatenate(parts, axis=1)


def local(factors, occupied_energy, virtual_energy, conserve, pair_lists):
    momenta, orbitals, virtuals, _, auxiliary = factors.shape
    share = virtuals // (LINE * CORES)
    start = lax.axis_index("occ") * share

    def outgoing(momentum):
        cut = lax.dynamic_slice(
            factors, (momentum, 0, start, 0, 0), (1, orbitals, share, 2, auxiliary)
        )
        cut = jnp.transpose(cut[0], (2, 0, 1, 3)).reshape(2 * orbitals * share, auxiliary)
        energy = lax.dynamic_slice(virtual_energy, (momentum, start), (1, share))
        head = jnp.pad(energy, ((0, HEAD - 1), (0, auxiliary - share)))
        return jnp.concatenate([cut, head], axis=0)

    line_pairs = line_pairs_of(pair_lists)
    straight = outgoing(0)
    relayed = outgoing(1)
    straight, relayed, line_pairs, factors = lax.optimization_barrier((straight, relayed, line_pairs, factors))
    cross_one = moved(straight, (3,), 1)
    cross_two = moved(straight, (2,), 2)
    hop_plus = lax.ppermute(relayed, ("ka", "occ"), ring_route(1))
    hop_minus = lax.ppermute(relayed, ("ka", "occ"), ring_route(-1))
    left = jnp.transpose(factors, (0, 1, 3, 2, 4)).reshape(momenta, orbitals, 2 * virtuals, auxiliary)
    other_pairs = lax.ppermute(line_pairs, "occ", [(i, i ^ 1) for i in range(LINE * CORES)])
    pairs = jnp.concatenate([line_pairs, other_pairs], axis=1)
    straight, hop_plus, hop_minus, left, pairs = lax.optimization_barrier(
        (straight, hop_plus, hop_minus, left, pairs)
    )
    up = moved(hop_plus, (0,), 0)
    back = moved(hop_minus, range(COLUMNS), -1)
    near_one = moved(straight, (0, 1, 2), 1)
    straight, cross_one, cross_two, near_one = lax.optimization_barrier((straight, cross_one, cross_two, near_one))
    late_two = moved(straight, (3,), 2)
    near_two = moved(straight, (0, 1), 2)

    own_energy = virtual_energy.astype(jnp.float32)[:, None, :]
    core = lax.axis_index("occ") % CORES
    column = lax.axis_index("ka") % COLUMNS
    chosen = (conserve[0][:, None] + jnp.arange(momenta, dtype=jnp.int32)[None, :]) % momenta

    def density(round_index, momentum, mates, source, before, swapped):
        flags = jnp.stack([source.astype(jnp.int32), core.astype(jnp.int32), swapped])
        return piece_density(
            chosen[round_index, momentum].reshape(1), pairs[round_index], flags,
            occupied_energy, left, own_energy, mates, before,
        )

    zero = jnp.int32(0)
    early_a = density(0, 0, (cross_one, near_one), column != 0, (), zero)
    early_b = density(0, 1, (up, hop_plus), column != 0, (), zero)
    before = (*early_a, *early_b)
    late_b = density(1, 1, (back,), zero, before, (chosen[0, 0] != chosen[1, 1]).astype(jnp.int32))
    source = jnp.clip(column, 0, 2)
    late_a = density(
        1, 0, (cross_two, late_two, near_two), source, before, (chosen[0, 0] != chosen[1, 0]).astype(jnp.int32)
    )
    of_b = summed(*late_b)
    of_a = summed(*late_a)
    stacked = jnp.stack([of_a, of_b])
    result = jnp.where(chosen[1, 0] == 0, stacked, stacked[::-1])
    return jnp.transpose(result, (0, 2, 1, 3))


def ring_route(by):
    pairs = []
    for row in range(ROWS):
        for column in range(COLUMNS):
            for place in range(LINE):
                for core in range(CORES):
                    pairs.append(
                        (
                            device_index(row, column, place, core),
                            device_index(row, (column + by) % COLUMNS, place, core),
                        )
                    )
    return pairs


def solution(mesh):
    in_specs = (
        P("ka", None, None, None, None),
        P(),
        P("ka", None),
        P("ka", None),
        P(None, "occ", None),
    )
    out_specs = P("ka", "occ", None, None)
    return jax.shard_map(local, mesh=mesh, in_specs=in_specs, out_specs=out_specs, check_vma=False)
```

```python
import functools

import jax
import jax.numpy as jnp
from jax import lax
from jax.experimental import pallas as pl
from jax.experimental.pallas import tpu as pltpu
from jax.sharding import PartitionSpec as P

ROWS, COLUMNS, LINE, CORES = 8, 4, 4, 2
HEAD = 8


def device_index(row, column, place, core):
    return ((row % ROWS) * COLUMNS + column) * LINE * CORES + place * CORES + core


def moved(array, moves):
    pairs = []
    for row in range(ROWS):
        for column, (goal, crosses) in moves.items():
            for place in range(LINE):
                for core in range(CORES):
                    source = device_index(row, column, place, core)
                    end = LINE - 1 - place if crosses else place
                    pairs.append((source, device_index(row + crosses, goal, end, core)))
    return lax.ppermute(array, ("ka", "occ"), pairs)


def piece_kernel(
    sources, before_count, kind, order, conserve, pairs, here, occupied, own_energy, left, *refs
):
    mates, refs = refs[:sources], refs[sources:]
    before, refs = refs[:before_count], refs[before_count:]
    outs, refs = refs[:-8], refs[-8:]
    piece, own, products, combined, rounded, turned, total, arrived = refs
    orbitals = products.shape[0]
    virtuals = products.shape[3]
    rows = products.shape[2]
    share = rows // (2 * orbitals)
    devices, _, each, _ = pairs.shape
    count = devices * each
    column = here[0]
    core = here[1]

    def by_column(values):
        result = jnp.int32(values[-1])
        for number in range(len(values) - 2, -1, -1):
            result = jnp.where(column == number, jnp.int32(values[number]), result)
        return result

    round_index = by_column(order[0])
    momentum = by_column(order[1])
    source = by_column(order[2])
    mine = lax.rem(conserve[0, round_index] + momentum, jnp.int32(2))

    def copy_of(orbital):
        return pltpu.make_async_copy(left.at[mine, orbital], own.at[orbital], arrived.at[orbital])

    for orbital in range(orbitals):
        copy_of(orbital).start()
    for number, mate in enumerate(mates):

        @pl.when(source == number)
        def _():
            piece[...] = mate[...]

    contract = (((1,), (1,)), ((), ()))
    for orbital in range(orbitals):
        copy_of(orbital).wait()
        for part in range(2):
            products[orbital, part] = lax.dot_general(
                piece[:rows],
                own[orbital, part * virtuals : (part + 1) * virtuals],
                contract,
                preferred_element_type=jnp.float32,
            )

    width = 2 * 128
    energy_row = piece[rows : rows + 1, :width].astype(jnp.float32)
    first_row = piece[rows + 1 : rows + 2, :width].astype(jnp.float32)
    lane = lax.broadcasted_iota(jnp.int32, (share, width), 1)
    row = lax.broadcasted_iota(jnp.int32, (share, width), 0)
    wanted = (lane - row).astype(jnp.float32) == jnp.broadcast_to(first_row, (share, width))
    spread = jnp.broadcast_to(energy_row, (share, width))
    energy_mate = jnp.sum(jnp.where(wanted, spread, 0.0), axis=1, keepdims=True)
    energy_sum = own_energy[mine] + energy_mate

    def exchange(lead, trail):
        top = pl.ds(pl.multiple_of(trail * share, 8), share)
        bottom = pl.ds(pl.multiple_of((orbitals + trail) * share, 8), share)
        real = products[lead, 0, top] + products[lead, 1, bottom]
        imaginary = products[lead, 1, top] - products[lead, 0, bottom]
        return real, imaginary

    def one_pair(holder, number):
        lead = pairs[holder, round_index, number, 0]
        trail = pairs[holder, round_index, number, 1]
        inverse = 1.0 / (energy_sum - (occupied[lead] + occupied[trail]))
        real, imaginary = exchange(lead, trail)
        swapped_real, swapped_imaginary = exchange(trail, lead)
        real, imaginary = real * inverse, imaginary * inverse
        return (
            2.0 * real - swapped_real * inverse,
            2.0 * imaginary - swapped_imaginary * inverse,
            real,
            imaginary,
        )

    def two_pairs(index, carry):
        low = one_pair(index, 0)
        high = one_pair(index, 1)
        c_re, c_im, a_re, a_im = (
            jnp.concatenate([x, y], axis=0).astype(jnp.bfloat16) for x, y in zip(low, high)
        )
        top = pl.ds(pl.multiple_of(index * 2 * share, 16), 2 * share)
        bottom = pl.ds(pl.multiple_of((count + index * 2) * share, 16), 2 * share)
        combined[top] = c_re
        combined[bottom] = c_im
        rounded[top] = a_re
        rounded[bottom] = a_im
        turned[top] = -a_im
        turned[bottom] = a_re
        return carry

    lax.fori_loop(0, devices, two_pairs, 0)
    contract_rows = (((0,), (0,)), ((), ()))
    for part, right in enumerate((rounded, turned)):
        total[part] = lax.dot_general(
            combined[...], right[...], contract_rows, preferred_element_type=jnp.float32
        )
    done = lax.rem(conserve[0, 1], jnp.int32(2))
    for place in range(LINE):
        for number, offset in enumerate((core, 1 - core)):
            cut = pl.ds(pl.multiple_of((place * CORES + offset) * share, 8), share)
            value = total[:, cut]
            if kind == "first":
                for local_index in range(2):
                    outs[number][local_index, place] = jnp.where(mine == local_index, value, 0.0)
            elif kind == "second":
                for local_index in range(2):
                    outs[number][local_index, place] = before[number][local_index, place] + jnp.where(
                        mine == local_index, value, 0.0
                    )
            elif kind == "third":
                for slot, which in enumerate((done, 1 - done)):
                    outs[2 * slot + number][place] = before[number][which, place] + jnp.where(
                        mine == which, value, 0.0
                    )
            else:
                outs[number][place] = before[number][place] + value


def piece_density(kind, order, conserve, pairs, here, occupied, own_energy, left, mates, before):
    momenta, orbitals, both, auxiliary = left.shape
    virtuals = both // 2
    share = virtuals // (LINE * CORES)
    count = pairs.shape[0] * pairs.shape[2]
    rows = 2 * orbitals * share
    whole_block = jax.ShapeDtypeStruct((momenta, LINE, 2, share, virtuals), jnp.float32)
    block = jax.ShapeDtypeStruct((LINE, 2, share, virtuals), jnp.float32)
    out_shape = {
        "first": (whole_block,) * 2,
        "second": (whole_block,) * 2,
        "third": (block,) * 4,
        "fourth": (block,) * 2,
    }[kind]
    scalars = pl.BlockSpec(memory_space=pltpu.SMEM)
    whole = pl.BlockSpec(memory_space=pltpu.VMEM)
    return pl.pallas_call(
        functools.partial(piece_kernel, len(mates), len(before), kind, order),
        out_shape=out_shape,
        in_specs=[scalars] * 4
        + [whole, pl.BlockSpec(memory_space=pl.ANY)]
        + [whole] * (len(mates) + len(before)),
        out_specs=(whole,) * len(out_shape),
        scratch_shapes=[
            pltpu.VMEM((rows + HEAD, auxiliary), jnp.bfloat16),
            pltpu.VMEM((orbitals, both, auxiliary), jnp.bfloat16),
            pltpu.VMEM((orbitals, 2, rows, virtuals), jnp.float32),
            pltpu.VMEM((2 * count * share, virtuals), jnp.bfloat16),
            pltpu.VMEM((2 * count * share, virtuals), jnp.bfloat16),
            pltpu.VMEM((2 * count * share, virtuals), jnp.bfloat16),
            pltpu.VMEM((2, virtuals, virtuals), jnp.float32),
            pltpu.SemaphoreType.DMA((orbitals,)),
        ],
        compiler_params=pltpu.CompilerParams(vmem_limit_bytes=40 << 20),
        cost_estimate=pl.CostEstimate(
            flops=4 * rows * virtuals * auxiliary * orbitals + 8 * count * share * virtuals * virtuals,
            bytes_accessed=orbitals * both * auxiliary * 2 + 2 * rows * auxiliary,
            transcendentals=0,
        ),
    )(conserve, pairs, here, occupied, own_energy, left, *mates, *before)


def summed(keep, send):
    place = lax.axis_index("occ") // CORES
    devices = LINE * CORES
    held = keep + lax.ppermute(send, "occ", [(i, i ^ 1) for i in range(devices)])
    total = lax.dynamic_index_in_dim(held, place, 0, keepdims=False)
    for hop in range(1, LINE):
        part = lax.dynamic_index_in_dim(held, (place + hop) % LINE, 0, keepdims=False)
        ring = [(i, (i + CORES * hop) % devices) for i in range(devices)]
        total = total + lax.ppermute(part, "occ", ring)
    return total


def with_partner(array, reach):
    other = lax.ppermute(array, "occ", [(i, i ^ reach) for i in range(LINE * CORES)])
    return jnp.concatenate([array, other], axis=0)


def local(factors, occupied_energy, virtual_energy, conserve, pair_lists):
    momenta, orbitals, virtuals, _, auxiliary = factors.shape
    share = virtuals // (LINE * CORES)
    start = lax.axis_index("occ") * share
    column = lax.axis_index("ka") % COLUMNS
    here = jnp.stack([column, lax.axis_index("occ") % CORES]).astype(jnp.int32)

    def outgoing(momentum):
        cut = lax.dynamic_slice(
            factors, (momentum, 0, start, 0, 0), (1, orbitals, share, 2, auxiliary)
        )
        cut = jnp.transpose(cut[0], (2, 0, 1, 3)).reshape(2 * orbitals * share, auxiliary)
        energy = jnp.pad(virtual_energy[momentum : momentum + 1], ((0, 0), (0, auxiliary - virtuals)))
        first = jnp.broadcast_to(start.astype(jnp.bfloat16), (HEAD - 1, auxiliary))
        return jnp.concatenate([cut, energy, first], axis=0)

    pairs = with_partner(with_partner(pair_lists[None], CORES), 2 * CORES)
    m0 = outgoing(0)
    m1 = outgoing(1)
    mixed = jnp.where(column == 3, m1, m0)
    m0, m1, mixed, pairs, factors, here = lax.optimization_barrier((m0, m1, mixed, pairs, factors, here))
    one = moved(m0, {0: (1, False), 1: (2, False), 2: (3, False), 3: (0, True)})
    two = moved(mixed, {2: (0, True), 3: (1, False)})
    three = moved(m1, {0: (1, False), 1: (2, False), 2: (3, False)})
    left = jnp.transpose(factors, (0, 1, 3, 2, 4)).reshape(momenta, orbitals, 2 * virtuals, auxiliary)
    pairs = with_partner(pairs, 1)
    own_energy = virtual_energy.astype(jnp.float32)[:, None, :]
    four_out = jnp.where(column == 0, one, m1)
    five_out = jnp.where(column == 1, two, m1)
    four_out, five_out, one, two, three, left, pairs, m0, own_energy = lax.optimization_barrier(
        (four_out, five_out, one, two, three, left, pairs, m0, own_energy)
    )
    four = moved(four_out, {3: (0, True), 0: (1, False), 1: (3, False)})
    five = moved(five_out, {2: (0, True), 1: (1, True), 0: (2, False)})
    six = moved(m0, {0: (2, False), 1: (3, False)})

    def density(kind, order, mates, before):
        return piece_density(
            kind, order, conserve, pairs, here, occupied_energy, own_energy, left, mates, before
        )

    total = density("first", ((0,), (0,), (0,)), (one,), ())
    total = density("second", ((1, 0), (0, 1), (0, 1)), (two, three), total)
    keep_a, send_a, keep_b, send_b = density(
        "third", ((0, 1), (1, 0), (0, 0, 1)), (four, six), total
    )
    keep_b, send_b = density("fourth", ((1,), (1,), (0, 0, 0, 1)), (five, four), (keep_b, send_b))
    done = summed(keep_a, send_a)
    last = summed(keep_b, send_b)
    result = jnp.where(conserve[0, 1] % 2 == 0, jnp.stack([done, last]), jnp.stack([last, done]))
    return jnp.transpose(result, (0, 2, 1, 3))


def solution(mesh):
    in_specs = (
        P("ka", None, None, None, None),
        P(),
        P("ka", None),
        P("ka", None),
        P(None, "occ", None),
    )
    out_specs = P("ka", "occ", None, None)
    return jax.shard_map(local, mesh=mesh, in_specs=in_specs, out_specs=out_specs, check_vma=False)
```

```python
import functools

import jax
import jax.numpy as jnp
from jax import lax
from jax.experimental import pallas as pl
from jax.experimental.pallas import tpu as pltpu
from jax.sharding import PartitionSpec as P

ROWS, COLUMNS, LINE, CORES = 8, 4, 4, 2
HEAD = 8


def device_index(row, column, place, core):
    return ((row % ROWS) * COLUMNS + column) * LINE * CORES + place * CORES + core


def moved(array, moves):
    pairs = []
    for row in range(ROWS):
        for column, (goal, crosses) in moves.items():
            for place in range(LINE):
                for core in range(CORES):
                    source = device_index(row, column, place, core)
                    end = LINE - 1 - place if crosses else place
                    pairs.append((source, device_index(row + crosses, goal, end, core)))
    return lax.ppermute(array, ("ka", "occ"), pairs)


def finished(column, conserve):
    return jnp.where(column == 0, lax.rem(conserve[0, 0], 2), 1 - lax.rem(conserve[0, 1], 2))


def piece_kernel(
    sources, before_count, kind, order, conserve, pairs, here, occupied, own_energy, left, *refs
):
    mates, refs = refs[:sources], refs[sources:]
    before, refs = refs[:before_count], refs[before_count:]
    outs, refs = refs[:-6], refs[-6:]
    piece, products, combined, rounded, turned, total = refs
    orbitals = products.shape[0]
    virtuals = products.shape[3]
    rows = products.shape[2]
    share = rows // (2 * orbitals)
    devices, _, each, _ = pairs.shape
    count = devices * each
    column = here[0]
    core = here[1]

    def by_column(values):
        result = jnp.int32(values[-1])
        for number in range(len(values) - 2, -1, -1):
            result = jnp.where(column == number, jnp.int32(values[number]), result)
        return result

    round_index = by_column(order[0])
    momentum = by_column(order[1])
    source = by_column(order[2])
    mine = lax.rem(conserve[0, round_index] + momentum, jnp.int32(2))

    for number, mate in enumerate(mates):

        @pl.when(source == number)
        def _():
            piece[...] = mate[...]

    contract = (((1,), (1,)), ((), ()))
    for orbital in range(orbitals):
        for part in range(2):
            products[orbital, part] = lax.dot_general(
                piece[:rows],
                left[mine, orbital, part * virtuals : (part + 1) * virtuals],
                contract,
                preferred_element_type=jnp.float32,
            )

    width = 2 * 128
    energy_row = piece[rows : rows + 1, :width].astype(jnp.float32)
    first_row = piece[rows + 1 : rows + 2, :width].astype(jnp.float32)
    lane = lax.broadcasted_iota(jnp.int32, (share, width), 1)
    row = lax.broadcasted_iota(jnp.int32, (share, width), 0)
    wanted = (lane - row).astype(jnp.float32) == jnp.broadcast_to(first_row, (share, width))
    spread = jnp.broadcast_to(energy_row, (share, width))
    energy_mate = jnp.sum(jnp.where(wanted, spread, 0.0), axis=1, keepdims=True)
    energy_sum = own_energy[mine] + energy_mate

    def exchange(lead, trail):
        top = pl.ds(pl.multiple_of(trail * share, 8), share)
        bottom = pl.ds(pl.multiple_of((orbitals + trail) * share, 8), share)
        real = products[lead, 0, top] + products[lead, 1, bottom]
        imaginary = products[lead, 1, top] - products[lead, 0, bottom]
        return real, imaginary

    def one_pair(holder, number):
        lead = pairs[holder, round_index, number, 0]
        trail = pairs[holder, round_index, number, 1]
        inverse = 1.0 / (energy_sum - (occupied[lead] + occupied[trail]))
        real, imaginary = exchange(lead, trail)
        swapped_real, swapped_imaginary = exchange(trail, lead)
        real, imaginary = real * inverse, imaginary * inverse
        return (
            2.0 * real - swapped_real * inverse,
            2.0 * imaginary - swapped_imaginary * inverse,
            real,
            imaginary,
        )

    def two_pairs(index, carry):
        low = one_pair(index, 0)
        high = one_pair(index, 1)
        c_re, c_im, a_re, a_im = (
            jnp.concatenate([x, y], axis=0).astype(jnp.bfloat16) for x, y in zip(low, high)
        )
        top = pl.ds(pl.multiple_of(index * 2 * share, 16), 2 * share)
        bottom = pl.ds(pl.multiple_of((count + index * 2) * share, 16), 2 * share)
        combined[top] = c_re
        combined[bottom] = c_im
        rounded[top] = a_re
        rounded[bottom] = a_im
        turned[top] = -a_im
        turned[bottom] = a_re
        return carry

    lax.fori_loop(0, devices, two_pairs, 0)
    contract_rows = (((0,), (0,)), ((), ()))
    for part, right in enumerate((rounded, turned)):
        total[part] = lax.dot_general(
            combined[...], right[...], contract_rows, preferred_element_type=jnp.float32
        )
    done = finished(column, conserve)
    for place in range(LINE):
        for number, offset in enumerate((core, 1 - core)):
            cut = pl.ds(pl.multiple_of((place * CORES + offset) * share, 8), share)
            value = total[:, cut]
            if kind == "first":
                for local_index in range(2):
                    outs[number][local_index, place] = jnp.where(mine == local_index, value, 0.0)
            elif kind == "second":
                for local_index in range(2):
                    outs[number][local_index, place] = before[number][local_index, place] + jnp.where(
                        mine == local_index, value, 0.0
                    )
            elif kind == "third":
                for slot, which in enumerate((done, 1 - done)):
                    outs[2 * slot + number][place] = before[number][which, place] + jnp.where(
                        mine == which, value, 0.0
                    )
            else:
                outs[number][place] = before[number][place] + value


def piece_density(kind, order, conserve, pairs, here, occupied, own_energy, left, mates, before):
    momenta, orbitals, both, auxiliary = left.shape
    virtuals = both // 2
    share = virtuals // (LINE * CORES)
    count = pairs.shape[0] * pairs.shape[2]
    rows = 2 * orbitals * share
    whole_block = jax.ShapeDtypeStruct((momenta, LINE, 2, share, virtuals), jnp.float32)
    block = jax.ShapeDtypeStruct((LINE, 2, share, virtuals), jnp.float32)
    out_shape = {
        "first": (whole_block,) * 2,
        "second": (whole_block,) * 2,
        "third": (block,) * 4,
        "fourth": (block,) * 2,
    }[kind]
    scalars = pl.BlockSpec(memory_space=pltpu.SMEM)
    whole = pl.BlockSpec(memory_space=pltpu.VMEM)
    return pl.pallas_call(
        functools.partial(piece_kernel, len(mates), len(before), kind, order),
        out_shape=out_shape,
        in_specs=[scalars] * 4
        + [whole] * (2 + len(mates) + len(before)),
        out_specs=(whole,) * len(out_shape),
        scratch_shapes=[
            pltpu.VMEM((rows + HEAD, auxiliary), jnp.bfloat16),
            pltpu.VMEM((orbitals, 2, rows, virtuals), jnp.float32),
            pltpu.VMEM((2 * count * share, virtuals), jnp.bfloat16),
            pltpu.VMEM((2 * count * share, virtuals), jnp.bfloat16),
            pltpu.VMEM((2 * count * share, virtuals), jnp.bfloat16),
            pltpu.VMEM((2, virtuals, virtuals), jnp.float32),
        ],
        compiler_params=pltpu.CompilerParams(vmem_limit_bytes=40 << 20),
        cost_estimate=pl.CostEstimate(
            flops=4 * rows * virtuals * auxiliary * orbitals + 8 * count * share * virtuals * virtuals,
            bytes_accessed=orbitals * both * auxiliary * 2 + 2 * rows * auxiliary,
            transcendentals=0,
        ),
    )(conserve, pairs, here, occupied, own_energy, left, *mates, *before)


def summed(keep, send):
    place = lax.axis_index("occ") // CORES
    devices = LINE * CORES
    held = keep + lax.ppermute(send, "occ", [(i, i ^ 1) for i in range(devices)])
    total = lax.dynamic_index_in_dim(held, place, 0, keepdims=False)
    for hop in range(1, LINE):
        part = lax.dynamic_index_in_dim(held, (place + hop) % LINE, 0, keepdims=False)
        ring = [(i, (i + CORES * hop) % devices) for i in range(devices)]
        total = total + lax.ppermute(part, "occ", ring)
    return total


def with_partner(array, reach):
    other = lax.ppermute(array, "occ", [(i, i ^ reach) for i in range(LINE * CORES)])
    return jnp.concatenate([array, other], axis=0)


def local(factors, occupied_energy, virtual_energy, conserve, pair_lists):
    momenta, orbitals, virtuals, _, auxiliary = factors.shape
    share = virtuals // (LINE * CORES)
    start = lax.axis_index("occ") * share
    column = lax.axis_index("ka") % COLUMNS
    here = jnp.stack([column, lax.axis_index("occ") % CORES]).astype(jnp.int32)

    def outgoing(momentum):
        cut = lax.dynamic_slice(
            factors, (momentum, 0, start, 0, 0), (1, orbitals, share, 2, auxiliary)
        )
        cut = jnp.transpose(cut[0], (2, 0, 1, 3)).reshape(2 * orbitals * share, auxiliary)
        energy = jnp.pad(virtual_energy[momentum : momentum + 1], ((0, 0), (0, auxiliary - virtuals)))
        first = jnp.broadcast_to(start.astype(jnp.bfloat16), (HEAD - 1, auxiliary))
        return jnp.concatenate([cut, energy, first], axis=0)

    pairs = with_partner(with_partner(pair_lists[None], CORES), 2 * CORES)
    m0 = outgoing(0)
    m1 = outgoing(1)
    m0, m1, pairs, factors, here = lax.optimization_barrier((m0, m1, pairs, factors, here))
    plus = moved(m1, {c: ((c + 1) % COLUMNS, False) for c in range(COLUMNS)})
    minus = moved(m1, {c: ((c - 1) % COLUMNS, False) for c in range(COLUMNS)})
    left = jnp.transpose(factors, (0, 1, 3, 2, 4)).reshape(momenta, orbitals, 2 * virtuals, auxiliary)
    m0, left = lax.optimization_barrier((m0, left))
    cross_one = moved(m0, {3: (0, True)})
    cross_two = moved(m0, {2: (0, True)})
    pairs = with_partner(pairs, 1)
    own_energy = virtual_energy.astype(jnp.float32)[:, None, :]
    m0, plus, minus, pairs, own_energy = lax.optimization_barrier((m0, plus, minus, pairs, own_energy))
    up = moved(plus, {0: (0, True)})
    back = moved(minus, {0: (3, False), 1: (0, True), 2: (1, True), 3: (2, False)})
    near_one = moved(m0, {0: (1, False), 1: (2, False), 2: (3, False)})
    m0, cross_one, cross_two, near_one = lax.optimization_barrier((m0, cross_one, cross_two, near_one))
    onward = moved(cross_one, {0: (1, False)})
    near_two = moved(m0, {0: (2, False), 1: (3, False)})

    def density(kind, order, mates, before):
        return piece_density(
            kind, order, conserve, pairs, here, occupied_energy, own_energy, left, mates, before
        )

    total = density("first", ((0,), (0,), (0, 1)), (cross_one, near_one), ())
    total = density("second", ((1,), (1,), (0,)), (back,), total)
    keep_a, send_a, keep_b, send_b = density(
        "third", ((1, 0), (0, 1), (0, 1)), (cross_two, plus), total
    )
    keep_b, send_b = density(
        "fourth", ((0, 1), (1, 0), (0, 1, 2)), (up, onward, near_two), (keep_b, send_b)
    )
    done = summed(keep_a, send_a)
    last = summed(keep_b, send_b)
    done_first = finished(column, conserve) == 0
    result = jnp.where(done_first, jnp.stack([done, last]), jnp.stack([last, done]))
    return jnp.transpose(result, (0, 2, 1, 3))


def solution(mesh):
    in_specs = (
        P("ka", None, None, None, None),
        P(),
        P("ka", None),
        P("ka", None),
        P(None, "occ", None),
    )
    out_specs = P("ka", "occ", None, None)
    return jax.shard_map(local, mesh=mesh, in_specs=in_specs, out_specs=out_specs, check_vma=False)
```

```python
import functools

import jax
import jax.numpy as jnp
from jax import lax
from jax.experimental import pallas as pl
from jax.experimental.pallas import tpu as pltpu
from jax.sharding import PartitionSpec as P

ROWS, COLUMNS, LINE, CORES = 8, 4, 4, 2
HEAD = 8


def device_index(row, column, place, core):
    return ((row % ROWS) * COLUMNS + column) * LINE * CORES + place * CORES + core


def moved(array, moves):
    pairs = []
    for row in range(ROWS):
        for column, (goal, next_row) in moves.items():
            goal_row = next_row(row)
            for place in range(LINE):
                for core in range(CORES):
                    source = device_index(row, column, place, core)
                    end = place if (goal_row - row) % 2 == 0 else LINE - 1 - place
                    pairs.append((source, device_index(goal_row, goal, end, core)))
    return lax.ppermute(array, ("ka", "occ"), pairs)


def same(row):
    return row


def onto_next(row):
    return row + 1


def beside_next(row):
    return row + 2 * (row % 2)


def across(row):
    return row ^ 1


def piece_kernel(
    sources, before_count, order, conserve, pairs, here, occupied, own_energy, left, *refs
):
    mates, refs = refs[:sources], refs[sources:]
    before, refs = refs[:before_count], refs[before_count:]
    outs, refs = refs[:-6], refs[-6:]
    piece, products, combined, rounded, turned, total = refs
    orbitals = products.shape[0]
    virtuals = products.shape[3]
    rows = products.shape[2]
    share = rows // (2 * orbitals)
    devices, _, each, _ = pairs.shape
    count = devices * each
    column = here[0]
    core = here[1]

    def by_column(values):
        result = jnp.int32(values[-1])
        for number in range(len(values) - 2, -1, -1):
            result = jnp.where(column == number, jnp.int32(values[number]), result)
        return result

    round_index = by_column(order[0])
    momentum = by_column(order[1])
    source = by_column(order[2])
    mine = lax.rem(conserve[0, round_index] + momentum, jnp.int32(2))

    for number, mate in enumerate(mates):

        @pl.when(source == number)
        def _():
            piece[...] = mate[...]

    contract = (((1,), (1,)), ((), ()))
    for orbital in range(orbitals):
        for part in range(2):
            products[orbital, part] = lax.dot_general(
                piece[:rows],
                left[mine, orbital, part * virtuals : (part + 1) * virtuals],
                contract,
                preferred_element_type=jnp.float32,
            )

    width = 2 * 128
    energy_row = piece[rows : rows + 1, :width].astype(jnp.float32)
    first_row = piece[rows + 1 : rows + 2, :width].astype(jnp.float32)
    lane = lax.broadcasted_iota(jnp.int32, (share, width), 1)
    row = lax.broadcasted_iota(jnp.int32, (share, width), 0)
    wanted = (lane - row).astype(jnp.float32) == jnp.broadcast_to(first_row, (share, width))
    spread = jnp.broadcast_to(energy_row, (share, width))
    energy_mate = jnp.sum(jnp.where(wanted, spread, 0.0), axis=1, keepdims=True)
    energy_sum = own_energy[mine] + energy_mate

    def exchange(lead, trail):
        top = pl.ds(pl.multiple_of(trail * share, 8), share)
        bottom = pl.ds(pl.multiple_of((orbitals + trail) * share, 8), share)
        real = products[lead, 0, top] + products[lead, 1, bottom]
        imaginary = products[lead, 1, top] - products[lead, 0, bottom]
        return real, imaginary

    def one_pair(holder, number):
        lead = pairs[holder, round_index, number, 0]
        trail = pairs[holder, round_index, number, 1]
        inverse = 1.0 / (energy_sum - (occupied[lead] + occupied[trail]))
        real, imaginary = exchange(lead, trail)
        swapped_real, swapped_imaginary = exchange(trail, lead)
        real, imaginary = real * inverse, imaginary * inverse
        return (
            2.0 * real - swapped_real * inverse,
            2.0 * imaginary - swapped_imaginary * inverse,
            real,
            imaginary,
        )

    def two_pairs(index, carry):
        low = one_pair(index, 0)
        high = one_pair(index, 1)
        c_re, c_im, a_re, a_im = (
            jnp.concatenate([x, y], axis=0).astype(jnp.bfloat16) for x, y in zip(low, high)
        )
        top = pl.ds(pl.multiple_of(index * 2 * share, 16), 2 * share)
        bottom = pl.ds(pl.multiple_of((count + index * 2) * share, 16), 2 * share)
        combined[top] = c_re
        combined[bottom] = c_im
        rounded[top] = a_re
        rounded[bottom] = a_im
        turned[top] = -a_im
        turned[bottom] = a_re
        return carry

    lax.fori_loop(0, devices, two_pairs, 0)
    contract_rows = (((0,), (0,)), ((), ()))
    for part, right in enumerate((rounded, turned)):
        total[part] = lax.dot_general(
            combined[...], right[...], contract_rows, preferred_element_type=jnp.float32
        )
    for place in range(LINE):
        for number, offset in enumerate((core, 1 - core)):
            cut = pl.ds(pl.multiple_of((place * CORES + offset) * share, 8), share)
            value = total[:, cut]
            for local_index in range(2):
                added = jnp.where(mine == local_index, value, 0.0)
                if before:
                    added = added + before[number][place, local_index]
                outs[number][place, local_index] = added


def piece_density(order, conserve, pairs, here, occupied, own_energy, left, mates, before):
    momenta, orbitals, both, auxiliary = left.shape
    virtuals = both // 2
    share = virtuals // (LINE * CORES)
    count = pairs.shape[0] * pairs.shape[2]
    rows = 2 * orbitals * share
    out_shape = (jax.ShapeDtypeStruct((LINE, momenta, 2, share, virtuals), jnp.float32),) * 2
    scalars = pl.BlockSpec(memory_space=pltpu.SMEM)
    whole = pl.BlockSpec(memory_space=pltpu.VMEM)
    return pl.pallas_call(
        functools.partial(piece_kernel, len(mates), len(before), order),
        out_shape=out_shape,
        in_specs=[scalars] * 4
        + [whole] * (2 + len(mates) + len(before)),
        out_specs=(whole,) * len(out_shape),
        scratch_shapes=[
            pltpu.VMEM((rows + HEAD, auxiliary), jnp.bfloat16),
            pltpu.VMEM((orbitals, 2, rows, virtuals), jnp.float32),
            pltpu.VMEM((2 * count * share, virtuals), jnp.bfloat16),
            pltpu.VMEM((2 * count * share, virtuals), jnp.bfloat16),
            pltpu.VMEM((2 * count * share, virtuals), jnp.bfloat16),
            pltpu.VMEM((2, virtuals, virtuals), jnp.float32),
        ],
        compiler_params=pltpu.CompilerParams(vmem_limit_bytes=32 << 20),
        cost_estimate=pl.CostEstimate(
            flops=4 * rows * virtuals * auxiliary * orbitals + 8 * count * share * virtuals * virtuals,
            bytes_accessed=orbitals * both * auxiliary * 2 + 2 * rows * auxiliary,
            transcendentals=0,
        ),
    )(conserve, pairs, here, occupied, own_energy, left, *mates, *before)


def summed(keep, send):
    place = lax.axis_index("occ") // CORES
    devices = LINE * CORES
    held = keep + lax.ppermute(send, "occ", [(i, i ^ 1) for i in range(devices)])
    total = lax.dynamic_index_in_dim(held, place, 0, keepdims=False)
    for hop in range(1, LINE):
        part = lax.dynamic_index_in_dim(held, (place + hop) % LINE, 0, keepdims=False)
        ring = [(i, (i + CORES * hop) % devices) for i in range(devices)]
        total = total + lax.ppermute(part, "occ", ring)
    return total


def with_partner(array, reach):
    other = lax.ppermute(array, "occ", [(i, i ^ reach) for i in range(LINE * CORES)])
    return jnp.concatenate([array, other], axis=0)


def local(factors, occupied_energy, virtual_energy, conserve, pair_lists):
    momenta, orbitals, virtuals, _, auxiliary = factors.shape
    share = virtuals // (LINE * CORES)
    start = lax.axis_index("occ") * share
    column = lax.axis_index("ka") % COLUMNS
    here = jnp.stack([column, lax.axis_index("occ") % CORES]).astype(jnp.int32)

    def outgoing(momentum):
        cut = lax.dynamic_slice(
            factors, (momentum, 0, start, 0, 0), (1, orbitals, share, 2, auxiliary)
        )
        cut = jnp.transpose(cut[0], (2, 0, 1, 3)).reshape(2 * orbitals * share, auxiliary)
        energy = jnp.pad(virtual_energy[momentum : momentum + 1], ((0, 0), (0, auxiliary - virtuals)))
        first = jnp.broadcast_to(start.astype(jnp.bfloat16), (HEAD - 1, auxiliary))
        return jnp.concatenate([cut, energy, first], axis=0)

    pairs = with_partner(pair_lists[None], CORES)
    m0 = outgoing(0)
    m1 = outgoing(1)
    m0, m1, pairs, factors, here = lax.optimization_barrier((m0, m1, pairs, factors, here))
    plus = moved(m1, {0: (1, same), 1: (2, same), 2: (3, same), 3: (0, beside_next)})
    minus = moved(m1, {0: (3, same), 1: (0, same), 2: (1, beside_next), 3: (2, beside_next)})
    pairs = with_partner(pairs, 2 * CORES)
    left = jnp.transpose(factors, (0, 1, 3, 2, 4)).reshape(momenta, orbitals, 2 * virtuals, auxiliary)
    m0, left, pairs = lax.optimization_barrier((m0, left, pairs))
    cross_one = moved(m0, {3: (0, onto_next)})
    cross_two = moved(m0, {2: (0, onto_next)})
    pairs = with_partner(pairs, 1)
    own_energy = virtual_energy.astype(jnp.float32)[:, None, :]
    m0, plus, minus, pairs, own_energy = lax.optimization_barrier((m0, plus, minus, pairs, own_energy))
    up = moved(plus, {0: (0, across)})
    back = moved(minus, {0: (3, same), 1: (0, across), 2: (1, across), 3: (2, same)})
    near_one = moved(m0, {0: (1, same), 1: (2, same), 2: (3, same)})
    m0, cross_one, near_one = lax.optimization_barrier((m0, cross_one, near_one))
    onward = moved(cross_one, {0: (1, same)})
    near_two = moved(m0, {0: (2, same), 1: (3, same)})

    def density(order, mates, before):
        return piece_density(
            order, conserve, pairs, here, occupied_energy, own_energy, left, mates, before
        )

    total = density(((0,), (0,), (0, 1)), (cross_one, near_one), ())
    total = density(((1, 0), (0, 1), (0, 1)), (cross_two, plus), total)
    total = density(((1,), (1,), (0,)), (back,), total)
    total = density(((0, 1), (1, 0), (0, 1, 2)), (up, onward, near_two), total)
    return jnp.transpose(summed(*total), (0, 2, 1, 3))


def solution(mesh):
    in_specs = (
        P("ka", None, None, None, None),
        P(),
        P("ka", None),
        P("ka", None),
        P(None, "occ", None),
    )
    out_specs = P("ka", "occ", None, None)
    return jax.shard_map(local, mesh=mesh, in_specs=in_specs, out_specs=out_specs, check_vma=False)
```

```python
import functools

import jax
import jax.numpy as jnp
from jax import lax
from jax.experimental import pallas as pl
from jax.experimental.pallas import tpu as pltpu
from jax.sharding import PartitionSpec as P

ROWS, COLUMNS, LINE, CORES = 8, 4, 4, 2
HEAD = 8


def device_index(row, column, place, core):
    return ((row % ROWS) * COLUMNS + column) * LINE * CORES + place * CORES + core


def moved(array, moves):
    pairs = []
    for row in range(ROWS):
        for column, (goal, next_row) in moves.items():
            goal_row = next_row(row)
            for place in range(LINE):
                for core in range(CORES):
                    source = device_index(row, column, place, core)
                    end = place if (goal_row - row) % 2 == 0 else LINE - 1 - place
                    pairs.append((source, device_index(goal_row, goal, end, core)))
    return lax.ppermute(array, ("ka", "occ"), pairs)


def same(row):
    return row


def onto_next(row):
    return row + 1


def beside_next(row):
    return row + 2 * (row % 2)


def across(row):
    return row ^ 1


def piece_kernel(
    sources, before_count, orders, held, conserve, pairs, here, occupied, own_energy, left, *refs
):
    mates, refs = refs[:sources], refs[sources:]
    before, refs = refs[:before_count], refs[before_count:]
    outs, refs = refs[:-6], refs[-6:]
    piece, products, combined, rounded, turned, total = refs
    orbitals = products.shape[0]
    virtuals = products.shape[3]
    rows = products.shape[2]
    share = rows // (2 * orbitals)
    devices, _, each, _ = pairs.shape
    count = devices * each
    column = here[0]
    core = here[1]

    def by_column(values):
        result = jnp.int32(values[-1])
        for number in range(len(values) - 2, -1, -1):
            result = jnp.where(column == number, jnp.int32(values[number]), result)
        return result

    round_index = by_column(orders[-1][0])
    momentum = by_column(orders[-1][1])
    source = by_column(held)
    def own_index(round_index, momentum):
        return lax.rem(conserve[0, round_index] + momentum, jnp.int32(2))

    mine = own_index(round_index, momentum)
    earlier = [
        (before[2 * number : 2 * number + 2], own_index(by_column(rounds), by_column(parts)))
        for number, (rounds, parts) in enumerate(orders[:-1])
    ]

    for number, mate in enumerate(mates):

        @pl.when(source == number)
        def _():
            piece[...] = mate[...]

    contract = (((1,), (1,)), ((), ()))
    for orbital in range(orbitals):
        for part in range(2):
            products[orbital, part] = lax.dot_general(
                piece[:rows],
                left[mine, orbital, part * virtuals : (part + 1) * virtuals],
                contract,
                preferred_element_type=jnp.float32,
            )

    width = 2 * 128
    energy_row = piece[rows : rows + 1, :width].astype(jnp.float32)
    first_row = piece[rows + 1 : rows + 2, :width].astype(jnp.float32)
    lane = lax.broadcasted_iota(jnp.int32, (share, width), 1)
    row = lax.broadcasted_iota(jnp.int32, (share, width), 0)
    wanted = (lane - row).astype(jnp.float32) == jnp.broadcast_to(first_row, (share, width))
    spread = jnp.broadcast_to(energy_row, (share, width))
    energy_mate = jnp.sum(jnp.where(wanted, spread, 0.0), axis=1, keepdims=True)
    energy_sum = own_energy[mine] + energy_mate

    def exchange(lead, trail):
        top = pl.ds(pl.multiple_of(trail * share, 8), share)
        bottom = pl.ds(pl.multiple_of((orbitals + trail) * share, 8), share)
        real = products[lead, 0, top] + products[lead, 1, bottom]
        imaginary = products[lead, 1, top] - products[lead, 0, bottom]
        return real, imaginary

    def one_pair(holder, number):
        lead = pairs[holder, round_index, number, 0]
        trail = pairs[holder, round_index, number, 1]
        inverse = 1.0 / (energy_sum - (occupied[lead] + occupied[trail]))
        real, imaginary = exchange(lead, trail)
        swapped_real, swapped_imaginary = exchange(trail, lead)
        real, imaginary = real * inverse, imaginary * inverse
        return (
            2.0 * real - swapped_real * inverse,
            2.0 * imaginary - swapped_imaginary * inverse,
            real,
            imaginary,
        )

    def two_pairs(index, carry):
        low = one_pair(index, 0)
        high = one_pair(index, 1)
        c_re, c_im, a_re, a_im = (
            jnp.concatenate([x, y], axis=0).astype(jnp.bfloat16) for x, y in zip(low, high)
        )
        top = pl.ds(pl.multiple_of(index * 2 * share, 16), 2 * share)
        bottom = pl.ds(pl.multiple_of((count + index * 2) * share, 16), 2 * share)
        combined[top] = c_re
        combined[bottom] = c_im
        rounded[top] = a_re
        rounded[bottom] = a_im
        turned[top] = -a_im
        turned[bottom] = a_re
        return carry

    lax.fori_loop(0, devices, two_pairs, 0)
    contract_rows = (((0,), (0,)), ((), ()))
    for part, right in enumerate((rounded, turned)):
        total[part] = lax.dot_general(
            combined[...], right[...], contract_rows, preferred_element_type=jnp.float32
        )
    for place in range(LINE):
        for number, offset in enumerate((core, 1 - core)):
            cut = pl.ds(pl.multiple_of((place * CORES + offset) * share, 8), share)
            value = total[:, cut]
            if not earlier:
                outs[number][place] = value
                continue
            for local_index in range(2):
                added = jnp.where(mine == local_index, value, 0.0)
                for (term, which) in earlier:
                    added = added + jnp.where(which == local_index, term[number][place], 0.0)
                outs[number][place, local_index] = added


def piece_density(orders, held, conserve, pairs, here, occupied, own_energy, left, mates, before):
    momenta, orbitals, both, auxiliary = left.shape
    virtuals = both // 2
    share = virtuals // (LINE * CORES)
    count = pairs.shape[0] * pairs.shape[2]
    rows = 2 * orbitals * share
    leading = (LINE, momenta) if before else (LINE,)
    out_shape = (jax.ShapeDtypeStruct((*leading, 2, share, virtuals), jnp.float32),) * 2
    scalars = pl.BlockSpec(memory_space=pltpu.SMEM)
    whole = pl.BlockSpec(memory_space=pltpu.VMEM)
    return pl.pallas_call(
        functools.partial(piece_kernel, len(mates), len(before), orders, held),
        out_shape=out_shape,
        in_specs=[scalars] * 4
        + [whole] * (2 + len(mates) + len(before)),
        out_specs=(whole,) * len(out_shape),
        scratch_shapes=[
            pltpu.VMEM((rows + HEAD, auxiliary), jnp.bfloat16),
            pltpu.VMEM((orbitals, 2, rows, virtuals), jnp.float32),
            pltpu.VMEM((2 * count * share, virtuals), jnp.bfloat16),
            pltpu.VMEM((2 * count * share, virtuals), jnp.bfloat16),
            pltpu.VMEM((2 * count * share, virtuals), jnp.bfloat16),
            pltpu.VMEM((2, virtuals, virtuals), jnp.float32),
        ],
        compiler_params=pltpu.CompilerParams(vmem_limit_bytes=32 << 20),
        cost_estimate=pl.CostEstimate(
            flops=4 * rows * virtuals * auxiliary * orbitals + 8 * count * share * virtuals * virtuals,
            bytes_accessed=orbitals * both * auxiliary * 2 + 2 * rows * auxiliary,
            transcendentals=0,
        ),
    )(conserve, pairs, here, occupied, own_energy, left, *mates, *before)


def summed(keep, send):
    place = lax.axis_index("occ") // CORES
    devices = LINE * CORES
    held = keep + lax.ppermute(send, "occ", [(i, i ^ 1) for i in range(devices)])
    total = lax.dynamic_index_in_dim(held, place, 0, keepdims=False)
    for hop in range(1, LINE):
        part = lax.dynamic_index_in_dim(held, (place + hop) % LINE, 0, keepdims=False)
        ring = [(i, (i + CORES * hop) % devices) for i in range(devices)]
        total = total + lax.ppermute(part, "occ", ring)
    return total


def with_partner(array, reach):
    other = lax.ppermute(array, "occ", [(i, i ^ reach) for i in range(LINE * CORES)])
    return jnp.concatenate([array, other], axis=0)


def local(factors, occupied_energy, virtual_energy, conserve, pair_lists):
    momenta, orbitals, virtuals, _, auxiliary = factors.shape
    share = virtuals // (LINE * CORES)
    start = lax.axis_index("occ") * share
    column = lax.axis_index("ka") % COLUMNS
    here = jnp.stack([column, lax.axis_index("occ") % CORES]).astype(jnp.int32)

    def outgoing(momentum):
        cut = lax.dynamic_slice(
            factors, (momentum, 0, start, 0, 0), (1, orbitals, share, 2, auxiliary)
        )
        cut = jnp.transpose(cut[0], (2, 0, 1, 3)).reshape(2 * orbitals * share, auxiliary)
        energy = jnp.pad(virtual_energy[momentum : momentum + 1], ((0, 0), (0, auxiliary - virtuals)))
        first = jnp.broadcast_to(start.astype(jnp.bfloat16), (HEAD - 1, auxiliary))
        return jnp.concatenate([cut, energy, first], axis=0)

    pairs = with_partner(pair_lists[None], CORES)
    m0 = outgoing(0)
    m1 = outgoing(1)
    m0, m1, pairs, factors, here = lax.optimization_barrier((m0, m1, pairs, factors, here))
    plus = moved(m1, {0: (1, same), 1: (2, same), 2: (3, same), 3: (0, beside_next)})
    minus = moved(m1, {0: (3, same), 1: (0, same), 2: (1, beside_next), 3: (2, beside_next)})
    pairs = with_partner(pairs, 2 * CORES)
    m0, pairs, factors = lax.optimization_barrier((m0, pairs, factors))
    cross_one = moved(m0, {3: (0, onto_next)})
    cross_two = moved(m0, {2: (0, onto_next)})
    pairs = with_partner(pairs, 1)
    own_energy = virtual_energy.astype(jnp.float32)[:, None, :]
    m0, plus, minus, factors, pairs, own_energy = lax.optimization_barrier(
        (m0, plus, minus, factors, pairs, own_energy)
    )
    up = moved(plus, {0: (0, across)})
    back = moved(minus, {0: (3, same), 1: (0, across), 2: (1, across), 3: (2, same)})
    near_one = moved(m0, {0: (1, same), 1: (2, same), 2: (3, same)})
    left = jnp.transpose(factors, (0, 1, 3, 2, 4)).reshape(momenta, orbitals, 2 * virtuals, auxiliary)
    m0, cross_one, near_one, left = lax.optimization_barrier((m0, cross_one, near_one, left))
    onward = moved(cross_one, {0: (1, same)})
    near_two = moved(m0, {0: (2, same), 1: (3, same)})

    def density(orders, held, mates, before):
        return piece_density(
            orders, held, conserve, pairs, here, occupied_energy, own_energy, left, mates, before
        )

    orders = (((0,), (0,)), ((1, 0), (0, 1)), ((1,), (1,)), ((0, 1), (1, 0)))
    terms = density(orders[:1], (0, 1), (cross_one, near_one), ())
    *terms, cross_two, plus = lax.optimization_barrier((*terms, cross_two, plus))
    terms += density(orders[1:2], (0, 1), (cross_two, plus), ())
    *terms, back = lax.optimization_barrier((*terms, back))
    terms += density(orders[2:3], (0,), (back,), ())
    total = density(orders, (0, 1, 2), (up, onward, near_two), terms)
    return jnp.transpose(summed(*total), (0, 2, 1, 3))


def solution(mesh):
    in_specs = (
        P("ka", None, None, None, None),
        P(),
        P("ka", None),
        P("ka", None),
        P(None, "occ", None),
    )
    out_specs = P("ka", "occ", None, None)
    return jax.shard_map(local, mesh=mesh, in_specs=in_specs, out_specs=out_specs, check_vma=False)
```

```python
import functools

import jax
import jax.numpy as jnp
from jax import lax
from jax.experimental import pallas as pl
from jax.experimental.pallas import tpu as pltpu
from jax.sharding import PartitionSpec as P

ROWS, COLUMNS, LINE, CORES = 8, 4, 4, 2
HEAD = 8


def device_index(row, column, place, core):
    return ((row % ROWS) * COLUMNS + column) * LINE * CORES + place * CORES + core


def moved(array, moves):
    pairs = []
    for row in range(ROWS):
        for column, (goal, next_row) in moves.items():
            goal_row = next_row(row)
            for place in range(LINE):
                for core in range(CORES):
                    source = device_index(row, column, place, core)
                    end = place if (goal_row - row) % 2 == 0 else LINE - 1 - place
                    pairs.append((source, device_index(goal_row, goal, end, core)))
    return lax.ppermute(array, ("ka", "occ"), pairs)


def same(row):
    return row


def onto_next(row):
    return row + 1


def beside_next(row):
    return row + 2 * (row % 2)


def across(row):
    return row ^ 1


def piece_kernel(
    sources, before_count, orders, held, conserve, pairs, here, occupied, own_energy, left, *refs
):
    mates, refs = refs[:sources], refs[sources:]
    before, refs = refs[:before_count], refs[before_count:]
    outs, refs = refs[:-6], refs[-6:]
    piece, products, combined, rounded, turned, total = refs
    orbitals = products.shape[0]
    virtuals = products.shape[3]
    rows = products.shape[2]
    share = rows // (2 * orbitals)
    devices, _, each, _ = pairs.shape
    count = devices * each
    column = here[0]
    core = here[1]

    def by_column(values):
        result = jnp.int32(values[-1])
        for number in range(len(values) - 2, -1, -1):
            result = jnp.where(column == number, jnp.int32(values[number]), result)
        return result

    round_index = by_column(orders[-1][0])
    momentum = by_column(orders[-1][1])
    source = by_column(held)
    def own_index(round_index, momentum):
        return lax.rem(conserve[0, round_index] + momentum, jnp.int32(2))

    mine = own_index(round_index, momentum)
    earlier = [
        (before[2 * number : 2 * number + 2], own_index(by_column(rounds), by_column(parts)))
        for number, (rounds, parts) in enumerate(orders[:-1])
    ]

    for number, mate in enumerate(mates):

        @pl.when(source == number)
        def _():
            piece[...] = mate[...]

    contract = (((1,), (1,)), ((), ()))
    for orbital in range(orbitals):
        for part in range(2):
            products[orbital, part] = lax.dot_general(
                piece[:rows],
                left[mine, orbital, part * virtuals : (part + 1) * virtuals],
                contract,
                preferred_element_type=jnp.float32,
            )

    width = 2 * 128
    energy_row = piece[rows : rows + 1, :width].astype(jnp.float32)
    first_row = piece[rows + 1 : rows + 2, :width].astype(jnp.float32)
    lane = lax.broadcasted_iota(jnp.int32, (share, width), 1)
    row = lax.broadcasted_iota(jnp.int32, (share, width), 0)
    wanted = (lane - row).astype(jnp.float32) == jnp.broadcast_to(first_row, (share, width))
    spread = jnp.broadcast_to(energy_row, (share, width))
    energy_mate = jnp.sum(jnp.where(wanted, spread, 0.0), axis=1, keepdims=True)
    energy_sum = own_energy[mine] + energy_mate

    def exchange(lead, trail):
        top = pl.ds(pl.multiple_of(trail * share, 8), share)
        bottom = pl.ds(pl.multiple_of((orbitals + trail) * share, 8), share)
        real = products[lead, 0, top] + products[lead, 1, bottom]
        imaginary = products[lead, 1, top] - products[lead, 0, bottom]
        return real, imaginary

    def one_pair(holder, number):
        lead = pairs[holder, round_index, number, 0]
        trail = pairs[holder, round_index, number, 1]
        inverse = 1.0 / (energy_sum - (occupied[lead] + occupied[trail]))
        real, imaginary = exchange(lead, trail)
        swapped_real, swapped_imaginary = exchange(trail, lead)
        real, imaginary = real * inverse, imaginary * inverse
        return (
            2.0 * real - swapped_real * inverse,
            2.0 * imaginary - swapped_imaginary * inverse,
            real,
            imaginary,
        )

    def two_pairs(index, carry):
        low = one_pair(index, 0)
        high = one_pair(index, 1)
        c_re, c_im, a_re, a_im = (
            jnp.concatenate([x, y], axis=0).astype(jnp.bfloat16) for x, y in zip(low, high)
        )
        top = pl.ds(pl.multiple_of(index * 2 * share, 16), 2 * share)
        bottom = pl.ds(pl.multiple_of((count + index * 2) * share, 16), 2 * share)
        combined[top] = c_re
        combined[bottom] = c_im
        rounded[top] = a_re
        rounded[bottom] = a_im
        turned[top] = -a_im
        turned[bottom] = a_re
        return carry

    lax.fori_loop(0, devices, two_pairs, 0)
    contract_rows = (((0,), (0,)), ((), ()))
    for part, right in enumerate((rounded, turned)):
        total[part] = lax.dot_general(
            combined[...], right[...], contract_rows, preferred_element_type=jnp.float32
        )
    for place in range(LINE):
        for number, offset in enumerate((core, 1 - core)):
            cut = pl.ds(pl.multiple_of((place * CORES + offset) * share, 8), share)
            value = total[:, cut]
            if not earlier:
                outs[number][place] = value
                continue
            for local_index in range(2):
                added = jnp.where(mine == local_index, value, 0.0)
                for (term, which) in earlier:
                    added = added + jnp.where(which == local_index, term[number][place], 0.0)
                outs[number][place, local_index] = added


def piece_density(orders, held, conserve, pairs, here, occupied, own_energy, left, mates, before):
    momenta, orbitals, both, auxiliary = left.shape
    virtuals = both // 2
    share = virtuals // (LINE * CORES)
    count = pairs.shape[0] * pairs.shape[2]
    rows = 2 * orbitals * share
    leading = (LINE, momenta) if before else (LINE,)
    out_shape = (jax.ShapeDtypeStruct((*leading, 2, share, virtuals), jnp.float32),) * 2
    scalars = pl.BlockSpec(memory_space=pltpu.SMEM)
    whole = pl.BlockSpec(memory_space=pltpu.VMEM)
    return pl.pallas_call(
        functools.partial(piece_kernel, len(mates), len(before), orders, held),
        out_shape=out_shape,
        in_specs=[scalars] * 4
        + [whole] * (2 + len(mates) + len(before)),
        out_specs=(whole,) * len(out_shape),
        scratch_shapes=[
            pltpu.VMEM((rows + HEAD, auxiliary), jnp.bfloat16),
            pltpu.VMEM((orbitals, 2, rows, virtuals), jnp.float32),
            pltpu.VMEM((2 * count * share, virtuals), jnp.bfloat16),
            pltpu.VMEM((2 * count * share, virtuals), jnp.bfloat16),
            pltpu.VMEM((2 * count * share, virtuals), jnp.bfloat16),
            pltpu.VMEM((2, virtuals, virtuals), jnp.float32),
        ],
        compiler_params=pltpu.CompilerParams(vmem_limit_bytes=32 << 20),
        cost_estimate=pl.CostEstimate(
            flops=4 * rows * virtuals * auxiliary * orbitals + 8 * count * share * virtuals * virtuals,
            bytes_accessed=orbitals * both * auxiliary * 2 + 2 * rows * auxiliary,
            transcendentals=0,
        ),
    )(conserve, pairs, here, occupied, own_energy, left, *mates, *before)


def summed(keep, send):
    place = lax.axis_index("occ") // CORES
    devices = LINE * CORES
    held = keep + lax.ppermute(send, "occ", [(i, i ^ 1) for i in range(devices)])
    total = lax.dynamic_index_in_dim(held, place, 0, keepdims=False)
    for hop in range(1, LINE):
        part = lax.dynamic_index_in_dim(held, (place + hop) % LINE, 0, keepdims=False)
        ring = [(i, (i + CORES * hop) % devices) for i in range(devices)]
        total = total + lax.ppermute(part, "occ", ring)
    return total


def with_partner(array, reach):
    other = lax.ppermute(array, "occ", [(i, i ^ reach) for i in range(LINE * CORES)])
    return jnp.concatenate([array, other], axis=0)


def local(factors, occupied_energy, virtual_energy, conserve, pair_lists):
    momenta, orbitals, virtuals, _, auxiliary = factors.shape
    share = virtuals // (LINE * CORES)
    start = lax.axis_index("occ") * share
    column = lax.axis_index("ka") % COLUMNS
    here = jnp.stack([column, lax.axis_index("occ") % CORES]).astype(jnp.int32)

    def outgoing(momentum):
        cut = lax.dynamic_slice(
            factors, (momentum, 0, start, 0, 0), (1, orbitals, share, 2, auxiliary)
        )
        cut = jnp.transpose(cut[0], (2, 0, 1, 3)).reshape(2 * orbitals * share, auxiliary)
        energy = jnp.pad(virtual_energy[momentum : momentum + 1], ((0, 0), (0, auxiliary - virtuals)))
        first = jnp.broadcast_to(start.astype(jnp.bfloat16), (HEAD - 1, auxiliary))
        return jnp.concatenate([cut, energy, first], axis=0)

    pairs = with_partner(pair_lists[None], CORES)
    m0 = outgoing(0)
    m1 = outgoing(1)
    m0, m1, pairs, factors, here = lax.optimization_barrier((m0, m1, pairs, factors, here))
    plus = moved(m1, {0: (1, same), 1: (2, same), 2: (3, same), 3: (0, beside_next)})
    minus = moved(m1, {0: (3, same), 1: (0, same), 2: (1, beside_next), 3: (2, beside_next)})
    pairs = with_partner(pairs, 2 * CORES)
    m0, pairs, factors = lax.optimization_barrier((m0, pairs, factors))
    cross_one = moved(m0, {3: (0, onto_next)})
    cross_two = moved(m0, {2: (0, onto_next)})
    pairs = with_partner(pairs, 1)
    own_energy = virtual_energy.astype(jnp.float32)[:, None, :]
    m0, plus, minus, factors, pairs, own_energy = lax.optimization_barrier(
        (m0, plus, minus, factors, pairs, own_energy)
    )
    up = moved(plus, {0: (0, across)})
    back = moved(minus, {0: (3, same), 1: (0, across), 2: (1, across), 3: (2, same)})
    near_one = moved(m0, {0: (1, same), 1: (2, same), 2: (3, same)})
    left = jnp.transpose(factors, (0, 1, 3, 2, 4)).reshape(momenta, orbitals, 2 * virtuals, auxiliary)
    m0, cross_one, cross_two, left = lax.optimization_barrier((m0, cross_one, cross_two, left))
    onward = moved(cross_one, {0: (1, same)})
    near_two = moved(m0, {0: (2, same), 1: (3, same)})

    def density(orders, held, mates, before):
        return piece_density(
            orders, held, conserve, pairs, here, occupied_energy, own_energy, left, mates, before
        )

    orders = (((0,), (0,)), ((1, 0), (0, 1)), ((1,), (1,)), ((0, 1), (1, 0)))
    terms = density(orders[:1], (0, 1), (cross_one, near_one), ())
    *terms, cross_two, plus = lax.optimization_barrier((*terms, cross_two, plus))
    terms += density(orders[1:2], (0, 1), (cross_two, plus), ())
    *terms, back = lax.optimization_barrier((*terms, back))
    terms += density(orders[2:3], (0,), (back,), ())
    total = density(orders, (0, 1, 2), (up, onward, near_two), terms)
    return jnp.transpose(summed(*total), (0, 2, 1, 3))


def solution(mesh):
    in_specs = (
        P("ka", None, None, None, None),
        P(),
        P("ka", None),
        P("ka", None),
        P(None, "occ", None),
    )
    out_specs = P("ka", "occ", None, None)
    return jax.shard_map(local, mesh=mesh, in_specs=in_specs, out_specs=out_specs, check_vma=False)
```

```python
import functools

import jax
import jax.numpy as jnp
from jax import lax
from jax.experimental import pallas as pl
from jax.experimental.pallas import tpu as pltpu
from jax.sharding import PartitionSpec as P

ROWS, COLUMNS, LINE, CORES = 8, 4, 4, 2
HEAD = 8


def device_index(row, column, place, core):
    return ((row % ROWS) * COLUMNS + column) * LINE * CORES + place * CORES + core


def moved(array, moves):
    pairs = []
    for row in range(ROWS):
        for column, (goal, next_row) in moves.items():
            goal_row = next_row(row)
            for place in range(LINE):
                for core in range(CORES):
                    source = device_index(row, column, place, core)
                    end = place if (goal_row - row) % 2 == 0 else LINE - 1 - place
                    pairs.append((source, device_index(goal_row, goal, end, core)))
    return lax.ppermute(array, ("ka", "occ"), pairs)


def same(row):
    return row


def onto_next(row):
    return row + 1


def beside_next(row):
    return row + 2 * (row % 2)


def across(row):
    return row ^ 1


def piece_kernel(
    sources, before_count, orders, held, conserve, pairs, here, occupied, own_energy, left, *refs
):
    mates, refs = refs[:sources], refs[sources:]
    before, refs = refs[:before_count], refs[before_count:]
    outs, refs = refs[:-6], refs[-6:]
    piece, products, combined, rounded, turned, total = refs
    orbitals = products.shape[0]
    virtuals = products.shape[3]
    rows = products.shape[2]
    share = rows // (2 * orbitals)
    devices, _, each, _ = pairs.shape
    count = devices * each
    column = here[0]
    core = here[1]

    def by_column(values):
        result = jnp.int32(values[-1])
        for number in range(len(values) - 2, -1, -1):
            result = jnp.where(column == number, jnp.int32(values[number]), result)
        return result

    round_index = by_column(orders[-1][0])
    momentum = by_column(orders[-1][1])
    source = by_column(held)
    def own_index(round_index, momentum):
        return lax.rem(conserve[0, round_index] + momentum, jnp.int32(2))

    mine = own_index(round_index, momentum)
    earlier = [
        (before[2 * number : 2 * number + 2], own_index(by_column(rounds), by_column(parts)))
        for number, (rounds, parts) in enumerate(orders[:-1])
    ]

    for number, mate in enumerate(mates):

        @pl.when(source == number)
        def _():
            piece[...] = mate[...]

    contract = (((1,), (1,)), ((), ()))
    for orbital in range(orbitals):
        for part in range(2):
            products[orbital, part] = lax.dot_general(
                piece[:rows],
                left[mine, orbital, part * virtuals : (part + 1) * virtuals],
                contract,
                preferred_element_type=jnp.float32,
            )

    width = 2 * 128
    energy_row = piece[rows : rows + 1, :width].astype(jnp.float32)
    first_row = piece[rows + 1 : rows + 2, :width].astype(jnp.float32)
    lane = lax.broadcasted_iota(jnp.int32, (share, width), 1)
    row = lax.broadcasted_iota(jnp.int32, (share, width), 0)
    wanted = (lane - row).astype(jnp.float32) == jnp.broadcast_to(first_row, (share, width))
    spread = jnp.broadcast_to(energy_row, (share, width))
    energy_mate = jnp.sum(jnp.where(wanted, spread, 0.0), axis=1, keepdims=True)
    energy_sum = own_energy[mine] + energy_mate

    def exchange(lead, trail):
        top = pl.ds(pl.multiple_of(trail * share, 8), share)
        bottom = pl.ds(pl.multiple_of((orbitals + trail) * share, 8), share)
        real = products[lead, 0, top] + products[lead, 1, bottom]
        imaginary = products[lead, 1, top] - products[lead, 0, bottom]
        return real, imaginary

    def one_pair(holder, number):
        lead = pairs[holder, round_index, number, 0]
        trail = pairs[holder, round_index, number, 1]
        inverse = 1.0 / (energy_sum - (occupied[lead] + occupied[trail]))
        real, imaginary = exchange(lead, trail)
        swapped_real, swapped_imaginary = exchange(trail, lead)
        real, imaginary = real * inverse, imaginary * inverse
        return (
            2.0 * real - swapped_real * inverse,
            2.0 * imaginary - swapped_imaginary * inverse,
            real,
            imaginary,
        )

    def two_pairs(index, carry):
        low = one_pair(index, 0)
        high = one_pair(index, 1)
        c_re, c_im, a_re, a_im = (
            jnp.concatenate([x, y], axis=0).astype(jnp.bfloat16) for x, y in zip(low, high)
        )
        top = pl.ds(pl.multiple_of(index * 2 * share, 16), 2 * share)
        bottom = pl.ds(pl.multiple_of((count + index * 2) * share, 16), 2 * share)
        combined[top] = c_re
        combined[bottom] = c_im
        rounded[top] = a_re
        rounded[bottom] = a_im
        turned[top] = -a_im
        turned[bottom] = a_re
        return carry

    lax.fori_loop(0, devices, two_pairs, 0)
    contract_rows = (((0,), (0,)), ((), ()))
    for part, right in enumerate((rounded, turned)):
        total[part] = lax.dot_general(
            combined[...], right[...], contract_rows, preferred_element_type=jnp.float32
        )
    for place in range(LINE):
        for number, offset in enumerate((core, 1 - core)):
            cut = pl.ds(pl.multiple_of((place * CORES + offset) * share, 8), share)
            value = total[:, cut]
            if not earlier:
                outs[number][place] = value
                continue
            for local_index in range(2):
                added = jnp.where(mine == local_index, value, 0.0)
                for (term, which) in earlier:
                    added = added + jnp.where(which == local_index, term[number][place], 0.0)
                outs[number][place, local_index] = added


def piece_density(orders, held, conserve, pairs, here, occupied, own_energy, left, mates, before):
    momenta, orbitals, both, auxiliary = left.shape
    virtuals = both // 2
    share = virtuals // (LINE * CORES)
    count = pairs.shape[0] * pairs.shape[2]
    rows = 2 * orbitals * share
    leading = (LINE, momenta) if before else (LINE,)
    out_shape = (jax.ShapeDtypeStruct((*leading, 2, share, virtuals), jnp.float32),) * 2
    scalars = pl.BlockSpec(memory_space=pltpu.SMEM)
    whole = pl.BlockSpec(memory_space=pltpu.VMEM)
    return pl.pallas_call(
        functools.partial(piece_kernel, len(mates), len(before), orders, held),
        out_shape=out_shape,
        in_specs=[scalars] * 4
        + [whole] * (2 + len(mates) + len(before)),
        out_specs=(whole,) * len(out_shape),
        scratch_shapes=[
            pltpu.VMEM((rows + HEAD, auxiliary), jnp.bfloat16),
            pltpu.VMEM((orbitals, 2, rows, virtuals), jnp.float32),
            pltpu.VMEM((2 * count * share, virtuals), jnp.bfloat16),
            pltpu.VMEM((2 * count * share, virtuals), jnp.bfloat16),
            pltpu.VMEM((2 * count * share, virtuals), jnp.bfloat16),
            pltpu.VMEM((2, virtuals, virtuals), jnp.float32),
        ],
        compiler_params=pltpu.CompilerParams(vmem_limit_bytes=32 << 20),
        cost_estimate=pl.CostEstimate(
            flops=4 * rows * virtuals * auxiliary * orbitals + 8 * count * share * virtuals * virtuals,
            bytes_accessed=orbitals * both * auxiliary * 2 + 2 * rows * auxiliary,
            transcendentals=0,
        ),
    )(conserve, pairs, here, occupied, own_energy, left, *mates, *before)


def summed(keep, send):
    place = lax.axis_index("occ") // CORES
    devices = LINE * CORES
    held = keep + lax.ppermute(send, "occ", [(i, i ^ 1) for i in range(devices)])
    total = lax.dynamic_index_in_dim(held, place, 0, keepdims=False)
    for hop in range(1, LINE):
        part = lax.dynamic_index_in_dim(held, (place + hop) % LINE, 0, keepdims=False)
        ring = [(i, (i + CORES * hop) % devices) for i in range(devices)]
        total = total + lax.ppermute(part, "occ", ring)
    return total


def with_partner(array, reach):
    other = lax.ppermute(array, "occ", [(i, i ^ reach) for i in range(LINE * CORES)])
    return jnp.concatenate([array, other], axis=0)


def local(factors, occupied_energy, virtual_energy, conserve, pair_lists):
    momenta, orbitals, virtuals, _, auxiliary = factors.shape
    share = virtuals // (LINE * CORES)
    start = lax.axis_index("occ") * share
    column = lax.axis_index("ka") % COLUMNS
    here = jnp.stack([column, lax.axis_index("occ") % CORES]).astype(jnp.int32)

    def outgoing(momentum):
        cut = lax.dynamic_slice(
            factors, (momentum, 0, start, 0, 0), (1, orbitals, share, 2, auxiliary)
        )
        cut = jnp.transpose(cut[0], (2, 0, 1, 3)).reshape(2 * orbitals * share, auxiliary)
        energy = jnp.pad(virtual_energy[momentum : momentum + 1], ((0, 0), (0, auxiliary - virtuals)))
        first = jnp.broadcast_to(start.astype(jnp.bfloat16), (HEAD - 1, auxiliary))
        return jnp.concatenate([cut, energy, first], axis=0)

    pairs = with_partner(pair_lists[None], CORES)
    m0 = outgoing(0)
    m1 = outgoing(1)
    m0, m1, pairs, factors, here = lax.optimization_barrier((m0, m1, pairs, factors, here))
    plus = moved(m1, {0: (1, same), 1: (2, same), 2: (3, same), 3: (0, beside_next)})
    minus = moved(m1, {0: (3, same), 1: (0, same), 2: (1, beside_next), 3: (2, beside_next)})
    pairs = with_partner(pairs, 2 * CORES)
    m0, pairs, factors = lax.optimization_barrier((m0, pairs, factors))
    cross_one = moved(m0, {3: (0, onto_next)})
    two = moved(m0, {0: (2, same), 1: (3, same), 2: (0, onto_next)})
    pairs = with_partner(pairs, 1)
    own_energy = virtual_energy.astype(jnp.float32)[:, None, :]
    m0, plus, minus, factors, pairs, own_energy = lax.optimization_barrier(
        (m0, plus, minus, factors, pairs, own_energy)
    )
    up = moved(plus, {0: (0, across)})
    back = moved(minus, {0: (3, same), 1: (0, across), 2: (1, across), 3: (2, same)})
    near_one = moved(m0, {0: (1, same), 1: (2, same), 2: (3, same)})
    left = jnp.transpose(factors, (0, 1, 3, 2, 4)).reshape(momenta, orbitals, 2 * virtuals, auxiliary)
    cross_one, left = lax.optimization_barrier((cross_one, left))
    onward = moved(cross_one, {0: (1, same)})

    def density(orders, held, mates, before):
        return piece_density(
            orders, held, conserve, pairs, here, occupied_energy, own_energy, left, mates, before
        )

    orders = (((1, 0), (0, 1)), ((0,), (0,)), ((1,), (1,)), ((0, 1), (1, 0)))
    terms = density(orders[:1], (0, 1), (two, plus), ())
    *terms, cross_one, near_one = lax.optimization_barrier((*terms, cross_one, near_one))
    terms += density(orders[1:2], (0, 1), (cross_one, near_one), ())
    *terms, back = lax.optimization_barrier((*terms, back))
    terms += density(orders[2:3], (0,), (back,), ())
    total = density(orders, (0, 1, 2), (up, onward, two), terms)
    return jnp.transpose(summed(*total), (0, 2, 1, 3))


def solution(mesh):
    in_specs = (
        P("ka", None, None, None, None),
        P(),
        P("ka", None),
        P("ka", None),
        P(None, "occ", None),
    )
    out_specs = P("ka", "occ", None, None)
    return jax.shard_map(local, mesh=mesh, in_specs=in_specs, out_specs=out_specs, check_vma=False)
```

```python
import functools

import jax
import jax.numpy as jnp
from jax import lax
from jax.experimental import pallas as pl
from jax.experimental.pallas import tpu as pltpu
from jax.sharding import PartitionSpec as P

ROWS, COLUMNS, LINE, CORES = 8, 4, 4, 2
HEAD = 8


def device_index(row, column, place, core):
    return ((row % ROWS) * COLUMNS + column) * LINE * CORES + place * CORES + core


def moved(array, moves):
    pairs = []
    for row in range(ROWS):
        for column, (goal, next_row) in moves.items():
            goal_row = next_row(row)
            for place in range(LINE):
                for core in range(CORES):
                    source = device_index(row, column, place, core)
                    end = place if (goal_row - row) % 2 == 0 else LINE - 1 - place
                    pairs.append((source, device_index(goal_row, goal, end, core)))
    return lax.ppermute(array, ("ka", "occ"), pairs)


def same(row):
    return row


def onto_next(row):
    return row + 1


def beside_next(row):
    return row + 2 * (row % 2)


def across(row):
    return row ^ 1


def piece_kernel(
    sources, before_count, orders, held, conserve, pairs, here, occupied, own_energy, left, *refs
):
    mates, refs = refs[:sources], refs[sources:]
    before, refs = refs[:before_count], refs[before_count:]
    outs, refs = refs[:-6], refs[-6:]
    piece, products, combined, rounded, turned, total = refs
    orbitals = products.shape[0]
    virtuals = products.shape[3]
    rows = products.shape[2]
    share = rows // (2 * orbitals)
    devices, _, each, _ = pairs.shape
    count = devices * each
    column = here[0]
    core = here[1]

    def by_column(values):
        result = jnp.int32(values[-1])
        for number in range(len(values) - 2, -1, -1):
            result = jnp.where(column == number, jnp.int32(values[number]), result)
        return result

    round_index = by_column(orders[-1][0])
    momentum = by_column(orders[-1][1])
    source = by_column(held)
    def own_index(round_index, momentum):
        return lax.rem(conserve[0, round_index] + momentum, jnp.int32(2))

    mine = own_index(round_index, momentum)
    earlier = [
        (before[2 * number : 2 * number + 2], own_index(by_column(rounds), by_column(parts)))
        for number, (rounds, parts) in enumerate(orders[:-1])
    ]

    for number, mate in enumerate(mates):

        @pl.when(source == number)
        def _():
            piece[...] = mate[...]

    contract = (((1,), (1,)), ((), ()))
    for orbital in range(orbitals):
        for part in range(2):
            products[orbital, part] = lax.dot_general(
                piece[:rows],
                left[mine, orbital, part * virtuals : (part + 1) * virtuals],
                contract,
                preferred_element_type=jnp.float32,
            )

    width = 2 * 128
    energy_row = piece[rows : rows + 1, :width].astype(jnp.float32)
    first_row = piece[rows + 1 : rows + 2, :width].astype(jnp.float32)
    lane = lax.broadcasted_iota(jnp.int32, (share, width), 1)
    row = lax.broadcasted_iota(jnp.int32, (share, width), 0)
    wanted = (lane - row).astype(jnp.float32) == jnp.broadcast_to(first_row, (share, width))
    spread = jnp.broadcast_to(energy_row, (share, width))
    energy_mate = jnp.sum(jnp.where(wanted, spread, 0.0), axis=1, keepdims=True)
    energy_sum = own_energy[mine] + energy_mate

    def exchange(lead, trail):
        top = pl.ds(pl.multiple_of(trail * share, 8), share)
        bottom = pl.ds(pl.multiple_of((orbitals + trail) * share, 8), share)
        real = products[lead, 0, top] + products[lead, 1, bottom]
        imaginary = products[lead, 1, top] - products[lead, 0, bottom]
        return real, imaginary

    def one_pair(holder, number):
        lead = pairs[holder, round_index, number, 0]
        trail = pairs[holder, round_index, number, 1]
        inverse = 1.0 / (energy_sum - (occupied[lead] + occupied[trail]))
        real, imaginary = exchange(lead, trail)
        swapped_real, swapped_imaginary = exchange(trail, lead)
        real, imaginary = real * inverse, imaginary * inverse
        return (
            2.0 * real - swapped_real * inverse,
            2.0 * imaginary - swapped_imaginary * inverse,
            real,
            imaginary,
        )

    def two_pairs(index, carry):
        low = one_pair(index, 0)
        high = one_pair(index, 1)
        c_re, c_im, a_re, a_im = (
            jnp.concatenate([x, y], axis=0).astype(jnp.bfloat16) for x, y in zip(low, high)
        )
        top = pl.ds(pl.multiple_of(index * 2 * share, 16), 2 * share)
        bottom = pl.ds(pl.multiple_of((count + index * 2) * share, 16), 2 * share)
        combined[top] = c_re
        combined[bottom] = c_im
        rounded[top] = a_re
        rounded[bottom] = a_im
        turned[top] = -a_im
        turned[bottom] = a_re
        return carry

    lax.fori_loop(0, devices, two_pairs, 0)
    contract_rows = (((0,), (0,)), ((), ()))
    for part, right in enumerate((rounded, turned)):
        total[part] = lax.dot_general(
            combined[...], right[...], contract_rows, preferred_element_type=jnp.float32
        )
    for place in range(LINE):
        for number, offset in enumerate((core, 1 - core)):
            cut = pl.ds(pl.multiple_of((place * CORES + offset) * share, 8), share)
            value = total[:, cut]
            if not earlier:
                outs[number][place] = value
                continue
            for local_index in range(2):
                added = jnp.where(mine == local_index, value, 0.0)
                for (term, which) in earlier:
                    added = added + jnp.where(which == local_index, term[number][place], 0.0)
                outs[number][place, local_index] = added


def piece_density(orders, held, conserve, pairs, here, occupied, own_energy, left, mates, before):
    momenta, orbitals, both, auxiliary = left.shape
    virtuals = both // 2
    share = virtuals // (LINE * CORES)
    count = pairs.shape[0] * pairs.shape[2]
    rows = 2 * orbitals * share
    leading = (LINE, momenta) if before else (LINE,)
    out_shape = (jax.ShapeDtypeStruct((*leading, 2, share, virtuals), jnp.float32),) * 2
    scalars = pl.BlockSpec(memory_space=pltpu.SMEM)
    whole = pl.BlockSpec(memory_space=pltpu.VMEM)
    return pl.pallas_call(
        functools.partial(piece_kernel, len(mates), len(before), orders, held),
        out_shape=out_shape,
        in_specs=[scalars] * 4
        + [whole] * (2 + len(mates) + len(before)),
        out_specs=(whole,) * len(out_shape),
        scratch_shapes=[
            pltpu.VMEM((rows + HEAD, auxiliary), jnp.bfloat16),
            pltpu.VMEM((orbitals, 2, rows, virtuals), jnp.float32),
            pltpu.VMEM((2 * count * share, virtuals), jnp.bfloat16),
            pltpu.VMEM((2 * count * share, virtuals), jnp.bfloat16),
            pltpu.VMEM((2 * count * share, virtuals), jnp.bfloat16),
            pltpu.VMEM((2, virtuals, virtuals), jnp.float32),
        ],
        compiler_params=pltpu.CompilerParams(vmem_limit_bytes=32 << 20),
        cost_estimate=pl.CostEstimate(
            flops=4 * rows * virtuals * auxiliary * orbitals + 8 * count * share * virtuals * virtuals,
            bytes_accessed=orbitals * both * auxiliary * 2 + 2 * rows * auxiliary,
            transcendentals=0,
        ),
    )(conserve, pairs, here, occupied, own_energy, left, *mates, *before)


def summed(keep, send):
    place = lax.axis_index("occ") // CORES
    devices = LINE * CORES
    held = keep + lax.ppermute(send, "occ", [(i, i ^ 1) for i in range(devices)])
    total = lax.dynamic_index_in_dim(held, place, 0, keepdims=False)
    for hop in range(1, LINE):
        part = lax.dynamic_index_in_dim(held, (place + hop) % LINE, 0, keepdims=False)
        ring = [(i, (i + CORES * hop) % devices) for i in range(devices)]
        total = total + lax.ppermute(part, "occ", ring)
    return total


def with_partner(array, reach):
    other = lax.ppermute(array, "occ", [(i, i ^ reach) for i in range(LINE * CORES)])
    return jnp.concatenate([array, other], axis=0)


def local(factors, occupied_energy, virtual_energy, conserve, pair_lists):
    momenta, orbitals, virtuals, _, auxiliary = factors.shape
    share = virtuals // (LINE * CORES)
    start = lax.axis_index("occ") * share
    column = lax.axis_index("ka") % COLUMNS
    here = jnp.stack([column, lax.axis_index("occ") % CORES]).astype(jnp.int32)

    def outgoing(momentum):
        cut = lax.dynamic_slice(
            factors, (momentum, 0, start, 0, 0), (1, orbitals, share, 2, auxiliary)
        )
        cut = jnp.transpose(cut[0], (2, 0, 1, 3)).reshape(2 * orbitals * share, auxiliary)
        energy = jnp.pad(virtual_energy[momentum : momentum + 1], ((0, 0), (0, auxiliary - virtuals)))
        first = jnp.broadcast_to(start.astype(jnp.bfloat16), (HEAD - 1, auxiliary))
        return jnp.concatenate([cut, energy, first], axis=0)

    pairs = with_partner(pair_lists[None], CORES)
    m0 = outgoing(0)
    m1 = outgoing(1)
    m0, m1, pairs, factors, here = lax.optimization_barrier((m0, m1, pairs, factors, here))
    plus = moved(m1, {0: (1, same), 1: (2, same), 2: (3, same), 3: (0, beside_next)})
    minus = moved(m1, {0: (3, same), 1: (0, same), 2: (1, beside_next), 3: (2, beside_next)})
    pairs = with_partner(pairs, 2 * CORES)
    m0, pairs, factors = lax.optimization_barrier((m0, pairs, factors))
    cross_one = moved(m0, {3: (0, onto_next)})
    two = moved(m0, {0: (2, same), 2: (0, onto_next)})
    pairs = with_partner(pairs, 1)
    own_energy = virtual_energy.astype(jnp.float32)[:, None, :]
    m0, plus, minus, factors, pairs, own_energy = lax.optimization_barrier(
        (m0, plus, minus, factors, pairs, own_energy)
    )
    up = moved(plus, {0: (0, across)})
    back = moved(minus, {0: (3, same), 1: (0, across), 2: (1, across), 3: (2, same)})
    near_one = moved(m0, {0: (1, same), 1: (2, same), 2: (3, same)})
    left = jnp.transpose(factors, (0, 1, 3, 2, 4)).reshape(momenta, orbitals, 2 * virtuals, auxiliary)
    cross_one, left = lax.optimization_barrier((cross_one, left))
    onward = moved(jnp.where(column == 0, cross_one, m0), {0: (1, same), 1: (3, same)})

    def density(orders, held, mates, before):
        return piece_density(
            orders, held, conserve, pairs, here, occupied_energy, own_energy, left, mates, before
        )

    orders = (((1, 0), (0, 1)), ((0,), (0,)), ((1,), (1,)), ((0, 1), (1, 0)))
    terms = density(orders[:1], (0, 1), (two, plus), ())
    *terms, cross_one, near_one = lax.optimization_barrier((*terms, cross_one, near_one))
    terms += density(orders[1:2], (0, 1), (cross_one, near_one), ())
    *terms, back = lax.optimization_barrier((*terms, back))
    terms += density(orders[2:3], (0,), (back,), ())
    total = density(orders, (0, 1, 2, 1), (up, onward, two), terms)
    return jnp.transpose(summed(*total), (0, 2, 1, 3))


def solution(mesh):
    in_specs = (
        P("ka", None, None, None, None),
        P(),
        P("ka", None),
        P("ka", None),
        P(None, "occ", None),
    )
    out_specs = P("ka", "occ", None, None)
    return jax.shard_map(local, mesh=mesh, in_specs=in_specs, out_specs=out_specs, check_vma=False)
```

```python
import functools

import jax
import jax.numpy as jnp
from jax import lax
from jax.experimental import pallas as pl
from jax.experimental.pallas import tpu as pltpu
from jax.sharding import PartitionSpec as P

ROWS, COLUMNS, LINE, CORES = 8, 4, 4, 2
HEAD = 8


def device_index(row, column, place, core):
    return ((row % ROWS) * COLUMNS + column) * LINE * CORES + place * CORES + core


def moved(array, moves):
    pairs = []
    for row in range(ROWS):
        for column, (goal, next_row) in moves.items():
            goal_row = next_row(row)
            for place in range(LINE):
                for core in range(CORES):
                    source = device_index(row, column, place, core)
                    end = place if (goal_row - row) % 2 == 0 else LINE - 1 - place
                    pairs.append((source, device_index(goal_row, goal, end, core)))
    return lax.ppermute(array, ("ka", "occ"), pairs)


def same(row):
    return row


def onto_next(row):
    return row + 1


def beside_next(row):
    return row + 2 * (row % 2)


def across(row):
    return row ^ 1


def piece_kernel(
    sources, before_count, orders, held, conserve, pairs, here, occupied, own_energy, left, *refs
):
    mates, refs = refs[:sources], refs[sources:]
    before, refs = refs[:before_count], refs[before_count:]
    outs, refs = refs[:-6], refs[-6:]
    piece, products, combined, rounded, turned, total = refs
    orbitals = products.shape[0]
    virtuals = products.shape[3]
    rows = products.shape[2]
    share = rows // (2 * orbitals)
    devices, _, each, _ = pairs.shape
    count = devices * each
    column = here[0]
    core = here[1]

    def by_column(values):
        result = jnp.int32(values[-1])
        for number in range(len(values) - 2, -1, -1):
            result = jnp.where(column == number, jnp.int32(values[number]), result)
        return result

    round_index = by_column(orders[-1][0])
    momentum = by_column(orders[-1][1])
    source = by_column(held)
    def own_index(round_index, momentum):
        return lax.rem(conserve[0, round_index] + momentum, jnp.int32(2))

    mine = own_index(round_index, momentum)
    earlier = [
        (before[2 * number : 2 * number + 2], own_index(by_column(rounds), by_column(parts)))
        for number, (rounds, parts) in enumerate(orders[:-1])
    ]

    for number, mate in enumerate(mates):

        @pl.when(source == number)
        def _():
            piece[...] = mate[...]

    contract = (((1,), (1,)), ((), ()))
    for orbital in range(orbitals):
        for part in range(2):
            products[orbital, part] = lax.dot_general(
                piece[:rows],
                left[mine, orbital, part * virtuals : (part + 1) * virtuals],
                contract,
                preferred_element_type=jnp.float32,
            )

    width = 2 * 128
    energy_row = piece[rows : rows + 1, :width].astype(jnp.float32)
    first_row = piece[rows + 1 : rows + 2, :width].astype(jnp.float32)
    lane = lax.broadcasted_iota(jnp.int32, (share, width), 1)
    row = lax.broadcasted_iota(jnp.int32, (share, width), 0)
    wanted = (lane - row).astype(jnp.float32) == jnp.broadcast_to(first_row, (share, width))
    spread = jnp.broadcast_to(energy_row, (share, width))
    energy_mate = jnp.sum(jnp.where(wanted, spread, 0.0), axis=1, keepdims=True)
    energy_sum = own_energy[mine] + energy_mate

    def exchange(lead, trail):
        top = pl.ds(pl.multiple_of(trail * share, 8), share)
        bottom = pl.ds(pl.multiple_of((orbitals + trail) * share, 8), share)
        real = products[lead, 0, top] + products[lead, 1, bottom]
        imaginary = products[lead, 1, top] - products[lead, 0, bottom]
        return real, imaginary

    def one_pair(holder, number):
        lead = pairs[holder, round_index, number, 0]
        trail = pairs[holder, round_index, number, 1]
        inverse = 1.0 / (energy_sum - (occupied[lead] + occupied[trail]))
        real, imaginary = exchange(lead, trail)
        swapped_real, swapped_imaginary = exchange(trail, lead)
        real, imaginary = real * inverse, imaginary * inverse
        return (
            2.0 * real - swapped_real * inverse,
            2.0 * imaginary - swapped_imaginary * inverse,
            real,
            imaginary,
        )

    def two_pairs(index, carry):
        low = one_pair(index, 0)
        high = one_pair(index, 1)
        c_re, c_im, a_re, a_im = (
            jnp.concatenate([x, y], axis=0).astype(jnp.bfloat16) for x, y in zip(low, high)
        )
        top = pl.ds(pl.multiple_of(index * 2 * share, 16), 2 * share)
        bottom = pl.ds(pl.multiple_of((count + index * 2) * share, 16), 2 * share)
        combined[top] = c_re
        combined[bottom] = c_im
        rounded[top] = a_re
        rounded[bottom] = a_im
        turned[top] = -a_im
        turned[bottom] = a_re
        return carry

    lax.fori_loop(0, devices, two_pairs, 0)
    contract_rows = (((0,), (0,)), ((), ()))
    for part, right in enumerate((rounded, turned)):
        total[part] = lax.dot_general(
            combined[...], right[...], contract_rows, preferred_element_type=jnp.float32
        )
    for place in range(LINE):
        for number, offset in enumerate((core, 1 - core)):
            cut = pl.ds(pl.multiple_of((place * CORES + offset) * share, 8), share)
            value = total[:, cut]
            if not earlier:
                outs[number][place] = value
                continue
            for local_index in range(2):
                added = jnp.where(mine == local_index, value, 0.0)
                for (term, which) in earlier:
                    added = added + jnp.where(which == local_index, term[number][place], 0.0)
                outs[number][place, local_index] = added


def piece_density(orders, held, conserve, pairs, here, occupied, own_energy, left, mates, before):
    momenta, orbitals, both, auxiliary = left.shape
    virtuals = both // 2
    share = virtuals // (LINE * CORES)
    count = pairs.shape[0] * pairs.shape[2]
    rows = 2 * orbitals * share
    leading = (LINE, momenta) if before else (LINE,)
    out_shape = (jax.ShapeDtypeStruct((*leading, 2, share, virtuals), jnp.float32),) * 2
    scalars = pl.BlockSpec(memory_space=pltpu.SMEM)
    whole = pl.BlockSpec(memory_space=pltpu.VMEM)
    return pl.pallas_call(
        functools.partial(piece_kernel, len(mates), len(before), orders, held),
        out_shape=out_shape,
        in_specs=[scalars] * 4
        + [whole] * (2 + len(mates) + len(before)),
        out_specs=(whole,) * len(out_shape),
        scratch_shapes=[
            pltpu.VMEM((rows + HEAD, auxiliary), jnp.bfloat16),
            pltpu.VMEM((orbitals, 2, rows, virtuals), jnp.float32),
            pltpu.VMEM((2 * count * share, virtuals), jnp.bfloat16),
            pltpu.VMEM((2 * count * share, virtuals), jnp.bfloat16),
            pltpu.VMEM((2 * count * share, virtuals), jnp.bfloat16),
            pltpu.VMEM((2, virtuals, virtuals), jnp.float32),
        ],
        compiler_params=pltpu.CompilerParams(vmem_limit_bytes=32 << 20),
        cost_estimate=pl.CostEstimate(
            flops=4 * rows * virtuals * auxiliary * orbitals + 8 * count * share * virtuals * virtuals,
            bytes_accessed=orbitals * both * auxiliary * 2 + 2 * rows * auxiliary,
            transcendentals=0,
        ),
    )(conserve, pairs, here, occupied, own_energy, left, *mates, *before)


def summed(keep, send):
    place = lax.axis_index("occ") // CORES
    devices = LINE * CORES
    held = keep + lax.ppermute(send, "occ", [(i, i ^ 1) for i in range(devices)])
    total = lax.dynamic_index_in_dim(held, place, 0, keepdims=False)
    for hop in range(1, LINE):
        part = lax.dynamic_index_in_dim(held, (place + hop) % LINE, 0, keepdims=False)
        ring = [(i, (i + CORES * hop) % devices) for i in range(devices)]
        total = total + lax.ppermute(part, "occ", ring)
    return total


def with_partner(array, reach):
    other = lax.ppermute(array, "occ", [(i, i ^ reach) for i in range(LINE * CORES)])
    return jnp.concatenate([array, other], axis=0)


def local(factors, occupied_energy, virtual_energy, conserve, pair_lists):
    momenta, orbitals, virtuals, _, auxiliary = factors.shape
    share = virtuals // (LINE * CORES)
    start = lax.axis_index("occ") * share
    column = lax.axis_index("ka") % COLUMNS
    here = jnp.stack([column, lax.axis_index("occ") % CORES]).astype(jnp.int32)

    def outgoing(momentum):
        cut = lax.dynamic_slice(
            factors, (momentum, 0, start, 0, 0), (1, orbitals, share, 2, auxiliary)
        )
        cut = jnp.transpose(cut[0], (2, 0, 1, 3)).reshape(2 * orbitals * share, auxiliary)
        energy = jnp.pad(virtual_energy[momentum : momentum + 1], ((0, 0), (0, auxiliary - virtuals)))
        first = jnp.broadcast_to(start.astype(jnp.bfloat16), (HEAD - 1, auxiliary))
        return jnp.concatenate([cut, energy, first], axis=0)

    pairs = with_partner(pair_lists[None], CORES)
    m0 = outgoing(0)
    m1 = outgoing(1)
    m0, m1, pairs, factors, here = lax.optimization_barrier((m0, m1, pairs, factors, here))
    plus = moved(m1, {0: (1, same), 1: (2, same), 2: (3, same), 3: (0, beside_next)})
    minus = moved(m1, {0: (3, same), 1: (0, same), 2: (1, beside_next), 3: (2, beside_next)})
    pairs = with_partner(pairs, 2 * CORES)
    m0, pairs, factors = lax.optimization_barrier((m0, pairs, factors))
    cross_one = moved(m0, {3: (0, onto_next)})
    cross_two = moved(m0, {2: (0, onto_next)})
    pairs = with_partner(pairs, 1)
    own_energy = virtual_energy.astype(jnp.float32)[:, None, :]
    m0, plus, minus, factors, pairs, own_energy = lax.optimization_barrier(
        (m0, plus, minus, factors, pairs, own_energy)
    )
    up = moved(plus, {0: (0, across)})
    back = moved(minus, {0: (3, same), 1: (0, across), 2: (1, across), 3: (2, same)})
    near_one = moved(m0, {0: (1, same), 1: (2, same), 2: (3, same)})
    left = jnp.transpose(factors, (0, 1, 3, 2, 4)).reshape(momenta, orbitals, 2 * virtuals, auxiliary)
    m0, cross_one, near_one, left = lax.optimization_barrier((m0, cross_one, near_one, left))
    onward = moved(cross_one, {0: (1, same)})
    near_two = moved(m0, {0: (2, same), 1: (3, same)})

    def density(orders, held, mates, before):
        return piece_density(
            orders, held, conserve, pairs, here, occupied_energy, own_energy, left, mates, before
        )

    orders = (((0,), (0,)), ((1, 0), (0, 1)), ((0, 1), (1, 0)), ((1,), (1,)))
    terms = density(orders[:1], (0, 1), (cross_one, near_one), ())
    *terms, cross_two, plus = lax.optimization_barrier((*terms, cross_two, plus))
    terms += density(orders[1:2], (0, 1), (cross_two, plus), ())
    *terms, up, onward, near_two = lax.optimization_barrier((*terms, up, onward, near_two))
    terms += density(orders[2:3], (0, 1, 2), (up, onward, near_two), ())
    total = density(orders, (0,), (back,), terms)
    return jnp.transpose(summed(*total), (0, 2, 1, 3))


def solution(mesh):
    in_specs = (
        P("ka", None, None, None, None),
        P(),
        P("ka", None),
        P("ka", None),
        P(None, "occ", None),
    )
    out_specs = P("ka", "occ", None, None)
    return jax.shard_map(local, mesh=mesh, in_specs=in_specs, out_specs=out_specs, check_vma=False)
```

```python
import functools

import jax
import jax.numpy as jnp
from jax import lax
from jax.experimental import pallas as pl
from jax.experimental.pallas import tpu as pltpu
from jax.sharding import PartitionSpec as P

ROWS, COLUMNS, LINE, CORES = 8, 4, 4, 2
HEAD = 8


def device_index(row, column, place, core):
    return ((row % ROWS) * COLUMNS + column) * LINE * CORES + place * CORES + core


def moved(array, moves):
    pairs = []
    for row in range(ROWS):
        for column, (goal, next_row) in moves.items():
            goal_row = next_row(row)
            for place in range(LINE):
                for core in range(CORES):
                    source = device_index(row, column, place, core)
                    end = place if (goal_row - row) % 2 == 0 else LINE - 1 - place
                    pairs.append((source, device_index(goal_row, goal, end, core)))
    return lax.ppermute(array, ("ka", "occ"), pairs)


def same(row):
    return row


def onto_next(row):
    return row + 1


def beside_next(row):
    return row + 2 * (row % 2)


def across(row):
    return row ^ 1


def piece_kernel(
    sources, before_count, orders, held, conserve, pairs, here, occupied, own_energy, left, *refs
):
    mates, refs = refs[:sources], refs[sources:]
    before, refs = refs[:before_count], refs[before_count:]
    outs, refs = refs[:-6], refs[-6:]
    piece, products, combined, rounded, turned, total = refs
    orbitals = products.shape[0]
    virtuals = products.shape[3]
    rows = products.shape[2]
    share = rows // (2 * orbitals)
    devices, _, each, _ = pairs.shape
    count = devices * each
    column = here[0]
    core = here[1]

    def by_column(values):
        result = jnp.int32(values[-1])
        for number in range(len(values) - 2, -1, -1):
            result = jnp.where(column == number, jnp.int32(values[number]), result)
        return result

    round_index = by_column(orders[-1][0])
    momentum = by_column(orders[-1][1])
    source = by_column(held)
    def own_index(round_index, momentum):
        return lax.rem(conserve[0, round_index] + momentum, jnp.int32(2))

    mine = own_index(round_index, momentum)
    earlier = [
        (before[2 * number : 2 * number + 2], own_index(by_column(rounds), by_column(parts)))
        for number, (rounds, parts) in enumerate(orders[:-1])
    ]

    for number, mate in enumerate(mates):

        @pl.when(source == number)
        def _():
            piece[...] = mate[...]

    contract = (((1,), (1,)), ((), ()))
    for orbital in range(orbitals):
        for part in range(2):
            products[orbital, part] = lax.dot_general(
                piece[:rows],
                left[mine, orbital, part * virtuals : (part + 1) * virtuals],
                contract,
                preferred_element_type=jnp.float32,
            )

    width = 2 * 128
    energy_row = piece[rows : rows + 1, :width].astype(jnp.float32)
    first_row = piece[rows + 1 : rows + 2, :width].astype(jnp.float32)
    lane = lax.broadcasted_iota(jnp.int32, (share, width), 1)
    row = lax.broadcasted_iota(jnp.int32, (share, width), 0)
    wanted = (lane - row).astype(jnp.float32) == jnp.broadcast_to(first_row, (share, width))
    spread = jnp.broadcast_to(energy_row, (share, width))
    energy_mate = jnp.sum(jnp.where(wanted, spread, 0.0), axis=1, keepdims=True)
    energy_sum = own_energy[mine] + energy_mate

    def exchange(lead, trail):
        top = pl.ds(pl.multiple_of(trail * share, 8), share)
        bottom = pl.ds(pl.multiple_of((orbitals + trail) * share, 8), share)
        real = products[lead, 0, top] + products[lead, 1, bottom]
        imaginary = products[lead, 1, top] - products[lead, 0, bottom]
        return real, imaginary

    def one_pair(holder, number):
        lead = pairs[holder, round_index, number, 0]
        trail = pairs[holder, round_index, number, 1]
        inverse = 1.0 / (energy_sum - (occupied[lead] + occupied[trail]))
        real, imaginary = exchange(lead, trail)
        swapped_real, swapped_imaginary = exchange(trail, lead)
        real, imaginary = real * inverse, imaginary * inverse
        return (
            2.0 * real - swapped_real * inverse,
            2.0 * imaginary - swapped_imaginary * inverse,
            real,
            imaginary,
        )

    def two_pairs(index, carry):
        low = one_pair(index, 0)
        high = one_pair(index, 1)
        c_re, c_im, a_re, a_im = (
            jnp.concatenate([x, y], axis=0).astype(jnp.bfloat16) for x, y in zip(low, high)
        )
        top = pl.ds(pl.multiple_of(index * 2 * share, 16), 2 * share)
        bottom = pl.ds(pl.multiple_of((count + index * 2) * share, 16), 2 * share)
        combined[top] = c_re
        combined[bottom] = c_im
        rounded[top] = a_re
        rounded[bottom] = a_im
        turned[top] = -a_im
        turned[bottom] = a_re
        return carry

    lax.fori_loop(0, devices, two_pairs, 0)
    contract_rows = (((0,), (0,)), ((), ()))
    for part, right in enumerate((rounded, turned)):
        total[part] = lax.dot_general(
            combined[...], right[...], contract_rows, preferred_element_type=jnp.float32
        )
    for place in range(LINE):
        for number, offset in enumerate((core, 1 - core)):
            cut = pl.ds(pl.multiple_of((place * CORES + offset) * share, 8), share)
            value = total[:, cut]
            if not earlier:
                outs[number][place] = value
                continue
            for local_index in range(2):
                added = jnp.where(mine == local_index, value, 0.0)
                for (term, which) in earlier:
                    added = added + jnp.where(which == local_index, term[number][place], 0.0)
                outs[number][place, local_index] = added


def piece_density(orders, held, conserve, pairs, here, occupied, own_energy, left, mates, before):
    momenta, orbitals, both, auxiliary = left.shape
    virtuals = both // 2
    share = virtuals // (LINE * CORES)
    count = pairs.shape[0] * pairs.shape[2]
    rows = 2 * orbitals * share
    leading = (LINE, momenta) if before else (LINE,)
    out_shape = (jax.ShapeDtypeStruct((*leading, 2, share, virtuals), jnp.float32),) * 2
    scalars = pl.BlockSpec(memory_space=pltpu.SMEM)
    whole = pl.BlockSpec(memory_space=pltpu.VMEM)
    return pl.pallas_call(
        functools.partial(piece_kernel, len(mates), len(before), orders, held),
        out_shape=out_shape,
        in_specs=[scalars] * 4
        + [whole] * (2 + len(mates) + len(before)),
        out_specs=(whole,) * len(out_shape),
        scratch_shapes=[
            pltpu.VMEM((rows + HEAD, auxiliary), jnp.bfloat16),
            pltpu.VMEM((orbitals, 2, rows, virtuals), jnp.float32),
            pltpu.VMEM((2 * count * share, virtuals), jnp.bfloat16),
            pltpu.VMEM((2 * count * share, virtuals), jnp.bfloat16),
            pltpu.VMEM((2 * count * share, virtuals), jnp.bfloat16),
            pltpu.VMEM((2, virtuals, virtuals), jnp.float32),
        ],
        compiler_params=pltpu.CompilerParams(vmem_limit_bytes=32 << 20),
        cost_estimate=pl.CostEstimate(
            flops=4 * rows * virtuals * auxiliary * orbitals + 8 * count * share * virtuals * virtuals,
            bytes_accessed=orbitals * both * auxiliary * 2 + 2 * rows * auxiliary,
            transcendentals=0,
        ),
    )(conserve, pairs, here, occupied, own_energy, left, *mates, *before)


def summed(keep, send):
    place = lax.axis_index("occ") // CORES
    devices = LINE * CORES
    held = keep + lax.ppermute(send, "occ", [(i, i ^ 1) for i in range(devices)])
    total = lax.dynamic_index_in_dim(held, place, 0, keepdims=False)
    for hop in range(1, LINE):
        part = lax.dynamic_index_in_dim(held, (place + hop) % LINE, 0, keepdims=False)
        ring = [(i, (i + CORES * hop) % devices) for i in range(devices)]
        total = total + lax.ppermute(part, "occ", ring)
    return total


def with_partner(array, reach):
    other = lax.ppermute(array, "occ", [(i, i ^ reach) for i in range(LINE * CORES)])
    return jnp.concatenate([array, other], axis=0)


def local(factors, occupied_energy, virtual_energy, conserve, pair_lists):
    momenta, orbitals, virtuals, _, auxiliary = factors.shape
    share = virtuals // (LINE * CORES)
    start = lax.axis_index("occ") * share
    column = lax.axis_index("ka") % COLUMNS
    here = jnp.stack([column, lax.axis_index("occ") % CORES]).astype(jnp.int32)

    def outgoing(momentum):
        cut = lax.dynamic_slice(
            factors, (momentum, 0, start, 0, 0), (1, orbitals, share, 2, auxiliary)
        )
        cut = jnp.transpose(cut[0], (2, 0, 1, 3)).reshape(2 * orbitals * share, auxiliary)
        energy = jnp.pad(virtual_energy[momentum : momentum + 1], ((0, 0), (0, auxiliary - virtuals)))
        first = jnp.broadcast_to(start.astype(jnp.bfloat16), (HEAD - 1, auxiliary))
        return jnp.concatenate([cut, energy, first], axis=0)

    pairs = with_partner(pair_lists[None], CORES)
    m0 = outgoing(0)
    m1 = outgoing(1)
    m0, m1, pairs, factors, here = lax.optimization_barrier((m0, m1, pairs, factors, here))
    plus = moved(m1, {0: (1, same), 1: (2, same), 2: (3, same), 3: (0, beside_next)})
    minus = moved(m1, {0: (3, same), 1: (0, same), 2: (1, beside_next), 3: (2, beside_next)})
    pairs = with_partner(with_partner(pairs, 2 * CORES), 1)
    m0, pairs, factors = lax.optimization_barrier((m0, pairs, factors))
    cross_one = moved(m0, {3: (0, onto_next)})
    two = moved(m0, {0: (2, same), 2: (0, onto_next)})
    own_energy = virtual_energy.astype(jnp.float32)[:, None, :]
    m0, plus, minus, factors, pairs, own_energy = lax.optimization_barrier(
        (m0, plus, minus, factors, pairs, own_energy)
    )
    up = moved(plus, {0: (0, across)})
    back = moved(minus, {0: (3, same), 1: (0, across), 2: (1, across), 3: (2, same)})
    near_one = moved(m0, {0: (1, same), 1: (2, same), 2: (3, same)})
    left = jnp.transpose(factors, (0, 1, 3, 2, 4)).reshape(momenta, orbitals, 2 * virtuals, auxiliary)
    m0, cross_one, left = lax.optimization_barrier((m0, cross_one, left))
    onward = moved(jnp.where(column == 0, cross_one, m0), {0: (1, same), 1: (3, same)})

    def density(orders, held, mates, before):
        return piece_density(
            orders, held, conserve, pairs, here, occupied_energy, own_energy, left, mates, before
        )

    orders = (((0,), (0,)), ((1, 0), (0, 1)), ((0, 1), (1, 0)), ((1,), (1,)))
    terms = density(orders[:1], (0, 1), (cross_one, near_one), ())
    *terms, two, plus = lax.optimization_barrier((*terms, two, plus))
    terms += density(orders[1:2], (0, 1), (two, plus), ())
    *terms, up, onward = lax.optimization_barrier((*terms, up, onward))
    terms += density(orders[2:3], (0, 1, 2, 1), (up, onward, two), ())
    total = density(orders, (0,), (back,), terms)
    return jnp.transpose(summed(*total), (0, 2, 1, 3))


def solution(mesh):
    in_specs = (
        P("ka", None, None, None, None),
        P(),
        P("ka", None),
        P("ka", None),
        P(None, "occ", None),
    )
    out_specs = P("ka", "occ", None, None)
    return jax.shard_map(local, mesh=mesh, in_specs=in_specs, out_specs=out_specs, check_vma=False)
```

```python
import functools

import jax
import jax.numpy as jnp
from jax import lax
from jax.experimental import pallas as pl
from jax.experimental.pallas import tpu as pltpu
from jax.sharding import PartitionSpec as P

ROWS, COLUMNS, LINE, CORES = 8, 4, 4, 2
HEAD = 8


def device_index(row, column, place, core):
    return ((row % ROWS) * COLUMNS + column) * LINE * CORES + place * CORES + core


def moved(array, moves):
    pairs = []
    for row in range(ROWS):
        for column, (goal, next_row) in moves.items():
            goal_row = next_row(row)
            for place in range(LINE):
                for core in range(CORES):
                    source = device_index(row, column, place, core)
                    end = place if (goal_row - row) % 2 == 0 else LINE - 1 - place
                    pairs.append((source, device_index(goal_row, goal, end, core)))
    return lax.ppermute(array, ("ka", "occ"), pairs)


def same(row):
    return row


def onto_next(row):
    return row + 1


def beside_next(row):
    return row + 2 * (row % 2)


def across(row):
    return row ^ 1


def piece_kernel(
    sources, before_count, orders, held, conserve, pairs, here, occupied, own_energy, left, *refs
):
    mates, refs = refs[:sources], refs[sources:]
    before, refs = refs[:before_count], refs[before_count:]
    outs, refs = refs[:-6], refs[-6:]
    piece, products, combined, rounded, turned, total = refs
    orbitals = products.shape[0]
    virtuals = products.shape[3]
    rows = products.shape[2]
    share = rows // (2 * orbitals)
    devices, _, each, _ = pairs.shape
    count = devices * each
    column = here[0]
    core = here[1]

    def by_column(values):
        result = jnp.int32(values[-1])
        for number in range(len(values) - 2, -1, -1):
            result = jnp.where(column == number, jnp.int32(values[number]), result)
        return result

    round_index = by_column(orders[-1][0])
    momentum = by_column(orders[-1][1])
    source = by_column(held)
    def own_index(round_index, momentum):
        return lax.rem(conserve[0, round_index] + momentum, jnp.int32(2))

    mine = own_index(round_index, momentum)
    earlier = [
        (before[2 * number : 2 * number + 2], own_index(by_column(rounds), by_column(parts)))
        for number, (rounds, parts) in enumerate(orders[:-1])
    ]

    for number, mate in enumerate(mates):

        @pl.when(source == number)
        def _():
            piece[...] = mate[...]

    contract = (((1,), (1,)), ((), ()))
    for orbital in range(orbitals):
        for part in range(2):
            products[orbital, part] = lax.dot_general(
                piece[:rows],
                left[mine, orbital, part * virtuals : (part + 1) * virtuals],
                contract,
                preferred_element_type=jnp.float32,
            )

    width = 2 * 128
    energy_row = piece[rows : rows + 1, :width].astype(jnp.float32)
    first_row = piece[rows + 1 : rows + 2, :width].astype(jnp.float32)
    lane = lax.broadcasted_iota(jnp.int32, (share, width), 1)
    row = lax.broadcasted_iota(jnp.int32, (share, width), 0)
    wanted = (lane - row).astype(jnp.float32) == jnp.broadcast_to(first_row, (share, width))
    spread = jnp.broadcast_to(energy_row, (share, width))
    energy_mate = jnp.sum(jnp.where(wanted, spread, 0.0), axis=1, keepdims=True)
    energy_sum = own_energy[mine] + energy_mate

    def exchange(lead, trail):
        top = pl.ds(pl.multiple_of(trail * share, 8), share)
        bottom = pl.ds(pl.multiple_of((orbitals + trail) * share, 8), share)
        real = products[lead, 0, top] + products[lead, 1, bottom]
        imaginary = products[lead, 1, top] - products[lead, 0, bottom]
        return real, imaginary

    def one_pair(holder, number):
        lead = pairs[holder, round_index, number, 0]
        trail = pairs[holder, round_index, number, 1]
        inverse = 1.0 / (energy_sum - (occupied[lead] + occupied[trail]))
        real, imaginary = exchange(lead, trail)
        swapped_real, swapped_imaginary = exchange(trail, lead)
        real, imaginary = real * inverse, imaginary * inverse
        return (
            2.0 * real - swapped_real * inverse,
            2.0 * imaginary - swapped_imaginary * inverse,
            real,
            imaginary,
        )

    def two_pairs(index, carry):
        low = one_pair(index, 0)
        high = one_pair(index, 1)
        c_re, c_im, a_re, a_im = (
            jnp.concatenate([x, y], axis=0).astype(jnp.bfloat16) for x, y in zip(low, high)
        )
        top = pl.ds(pl.multiple_of(index * 2 * share, 16), 2 * share)
        bottom = pl.ds(pl.multiple_of((count + index * 2) * share, 16), 2 * share)
        combined[top] = c_re
        combined[bottom] = c_im
        rounded[top] = a_re
        rounded[bottom] = a_im
        turned[top] = -a_im
        turned[bottom] = a_re
        return carry

    lax.fori_loop(0, devices, two_pairs, 0)
    contract_rows = (((0,), (0,)), ((), ()))
    for part, right in enumerate((rounded, turned)):
        total[part] = lax.dot_general(
            combined[...], right[...], contract_rows, preferred_element_type=jnp.float32
        )
    for place in range(LINE):
        for number, offset in enumerate((core, 1 - core)):
            cut = pl.ds(pl.multiple_of((place * CORES + offset) * share, 8), share)
            value = total[:, cut]
            if not earlier:
                outs[number][place] = value
                continue
            for local_index in range(2):
                added = jnp.where(mine == local_index, value, 0.0)
                for (term, which) in earlier:
                    added = added + jnp.where(which == local_index, term[number][place], 0.0)
                outs[number][place, local_index] = added


def piece_density(orders, held, conserve, pairs, here, occupied, own_energy, left, mates, before):
    momenta, orbitals, both, auxiliary = left.shape
    virtuals = both // 2
    share = virtuals // (LINE * CORES)
    count = pairs.shape[0] * pairs.shape[2]
    rows = 2 * orbitals * share
    leading = (LINE, momenta) if before else (LINE,)
    out_shape = (jax.ShapeDtypeStruct((*leading, 2, share, virtuals), jnp.float32),) * 2
    scalars = pl.BlockSpec(memory_space=pltpu.SMEM)
    whole = pl.BlockSpec(memory_space=pltpu.VMEM)
    return pl.pallas_call(
        functools.partial(piece_kernel, len(mates), len(before), orders, held),
        out_shape=out_shape,
        in_specs=[scalars] * 4
        + [whole] * (2 + len(mates) + len(before)),
        out_specs=(whole,) * len(out_shape),
        scratch_shapes=[
            pltpu.VMEM((rows + HEAD, auxiliary), jnp.bfloat16),
            pltpu.VMEM((orbitals, 2, rows, virtuals), jnp.float32),
            pltpu.VMEM((2 * count * share, virtuals), jnp.bfloat16),
            pltpu.VMEM((2 * count * share, virtuals), jnp.bfloat16),
            pltpu.VMEM((2 * count * share, virtuals), jnp.bfloat16),
            pltpu.VMEM((2, virtuals, virtuals), jnp.float32),
        ],
        compiler_params=pltpu.CompilerParams(vmem_limit_bytes=32 << 20),
        cost_estimate=pl.CostEstimate(
            flops=4 * rows * virtuals * auxiliary * orbitals + 8 * count * share * virtuals * virtuals,
            bytes_accessed=orbitals * both * auxiliary * 2 + 2 * rows * auxiliary,
            transcendentals=0,
        ),
    )(conserve, pairs, here, occupied, own_energy, left, *mates, *before)


def summed(keep, send):
    place = lax.axis_index("occ") // CORES
    devices = LINE * CORES
    held = keep + lax.ppermute(send, "occ", [(i, i ^ 1) for i in range(devices)])
    total = lax.dynamic_index_in_dim(held, place, 0, keepdims=False)
    for hop in range(1, LINE):
        part = lax.dynamic_index_in_dim(held, (place + hop) % LINE, 0, keepdims=False)
        ring = [(i, (i + CORES * hop) % devices) for i in range(devices)]
        total = total + lax.ppermute(part, "occ", ring)
    return total


def with_partner(array, reach):
    other = lax.ppermute(array, "occ", [(i, i ^ reach) for i in range(LINE * CORES)])
    return jnp.concatenate([array, other], axis=0)


def local(factors, occupied_energy, virtual_energy, conserve, pair_lists):
    momenta, orbitals, virtuals, _, auxiliary = factors.shape
    share = virtuals // (LINE * CORES)
    start = lax.axis_index("occ") * share
    column = lax.axis_index("ka") % COLUMNS
    here = jnp.stack([column, lax.axis_index("occ") % CORES]).astype(jnp.int32)

    def outgoing(momentum):
        cut = lax.dynamic_slice(
            factors, (momentum, 0, start, 0, 0), (1, orbitals, share, 2, auxiliary)
        )
        cut = jnp.transpose(cut[0], (2, 0, 1, 3)).reshape(2 * orbitals * share, auxiliary)
        energy = jnp.pad(virtual_energy[momentum : momentum + 1], ((0, 0), (0, auxiliary - virtuals)))
        first = jnp.broadcast_to(start.astype(jnp.bfloat16), (HEAD - 1, auxiliary))
        return jnp.concatenate([cut, energy, first], axis=0)

    pairs = with_partner(pair_lists[None], CORES)
    m0 = outgoing(0)
    m1 = outgoing(1)
    m0, m1, pairs, factors, here = lax.optimization_barrier((m0, m1, pairs, factors, here))
    plus = moved(m1, {0: (1, same), 1: (2, same), 2: (3, same), 3: (0, beside_next)})
    minus = moved(m1, {0: (3, same), 1: (0, same), 2: (1, beside_next), 3: (2, beside_next)})
    pairs = with_partner(with_partner(pairs, 2 * CORES), 1)
    m0, pairs, factors = lax.optimization_barrier((m0, pairs, factors))
    cross_one = moved(m0, {3: (0, onto_next)})
    two = moved(m0, {0: (2, same), 2: (0, onto_next)})
    own_energy = virtual_energy.astype(jnp.float32)[:, None, :]
    m0, plus, minus, factors, pairs, own_energy = lax.optimization_barrier(
        (m0, plus, minus, factors, pairs, own_energy)
    )
    up = moved(plus, {0: (0, across)})
    back = moved(minus, {0: (3, same), 1: (0, across), 2: (1, across), 3: (2, same)})
    near_one = moved(m0, {0: (1, same), 1: (2, same), 2: (3, same)})
    left = jnp.transpose(factors, (0, 1, 3, 2, 4)).reshape(momenta, orbitals, 2 * virtuals, auxiliary)
    m0, cross_one, left = lax.optimization_barrier((m0, cross_one, left))
    onward = moved(jnp.where(column == 0, cross_one, m0), {0: (1, same), 1: (3, same)})

    def density(orders, held, mates, before):
        return piece_density(
            orders, held, conserve, pairs, here, occupied_energy, own_energy, left, mates, before
        )

    orders = (((1, 0), (0, 1)), ((0,), (0,)), ((0, 1), (1, 0)), ((1,), (1,)))
    terms = density(orders[:1], (0, 1), (two, plus), ())
    *terms, cross_one, near_one = lax.optimization_barrier((*terms, cross_one, near_one))
    terms += density(orders[1:2], (0, 1), (cross_one, near_one), ())
    *terms, up, onward = lax.optimization_barrier((*terms, up, onward))
    terms += density(orders[2:3], (0, 1, 2, 1), (up, onward, two), ())
    total = density(orders, (0,), (back,), terms)
    return jnp.transpose(summed(*total), (0, 2, 1, 3))


def solution(mesh):
    in_specs = (
        P("ka", None, None, None, None),
        P(),
        P("ka", None),
        P("ka", None),
        P(None, "occ", None),
    )
    out_specs = P("ka", "occ", None, None)
    return jax.shard_map(local, mesh=mesh, in_specs=in_specs, out_specs=out_specs, check_vma=False)
```

```python
import functools

import jax
import jax.numpy as jnp
from jax import lax
from jax.experimental import pallas as pl
from jax.experimental.pallas import tpu as pltpu
from jax.sharding import PartitionSpec as P

ROWS, COLUMNS, LINE, CORES = 8, 4, 4, 2
HEAD = 8


def device_index(row, column, place, core):
    return ((row % ROWS) * COLUMNS + column) * LINE * CORES + place * CORES + core


def moved(array, moves):
    pairs = []
    for row in range(ROWS):
        for column, (goal, next_row) in moves.items():
            goal_row = next_row(row)
            for place in range(LINE):
                for core in range(CORES):
                    source = device_index(row, column, place, core)
                    end = place if (goal_row - row) % 2 == 0 else LINE - 1 - place
                    pairs.append((source, device_index(goal_row, goal, end, core)))
    return lax.ppermute(array, ("ka", "occ"), pairs)


def same(row):
    return row


def onto_next(row):
    return row + 1


def beside_next(row):
    return row + 2 * (row % 2)


def across(row):
    return row ^ 1


def piece_kernel(
    sources, before_count, orders, held, conserve, pairs, here, occupied, own_energy, left, *refs
):
    mates, refs = refs[:sources], refs[sources:]
    before, refs = refs[:before_count], refs[before_count:]
    outs, refs = refs[:-6], refs[-6:]
    piece, products, combined, rounded, turned, total = refs
    orbitals = products.shape[0]
    virtuals = products.shape[3]
    rows = products.shape[2]
    share = rows // (2 * orbitals)
    devices, _, each, _ = pairs.shape
    count = devices * each
    column = here[0]
    core = here[1]

    def by_column(values):
        result = jnp.int32(values[-1])
        for number in range(len(values) - 2, -1, -1):
            result = jnp.where(column == number, jnp.int32(values[number]), result)
        return result

    round_index = by_column(orders[-1][0])
    momentum = by_column(orders[-1][1])
    source = by_column(held)
    def own_index(round_index, momentum):
        return lax.rem(conserve[0, round_index] + momentum, jnp.int32(2))

    mine = own_index(round_index, momentum)
    earlier = [
        (before[2 * number : 2 * number + 2], own_index(by_column(rounds), by_column(parts)))
        for number, (rounds, parts) in enumerate(orders[:-1])
    ]

    for number, mate in enumerate(mates):

        @pl.when(source == number)
        def _():
            piece[...] = mate[...]

    contract = (((1,), (1,)), ((), ()))
    for orbital in range(orbitals):
        for part in range(2):
            products[orbital, part] = lax.dot_general(
                piece[:rows],
                left[mine, orbital, part * virtuals : (part + 1) * virtuals],
                contract,
                preferred_element_type=jnp.float32,
            )

    width = 2 * 128
    energy_row = piece[rows : rows + 1, :width].astype(jnp.float32)
    first_row = piece[rows + 1 : rows + 2, :width].astype(jnp.float32)
    lane = lax.broadcasted_iota(jnp.int32, (share, width), 1)
    row = lax.broadcasted_iota(jnp.int32, (share, width), 0)
    wanted = (lane - row).astype(jnp.float32) == jnp.broadcast_to(first_row, (share, width))
    spread = jnp.broadcast_to(energy_row, (share, width))
    energy_mate = jnp.sum(jnp.where(wanted, spread, 0.0), axis=1, keepdims=True)
    energy_sum = own_energy[mine] + energy_mate

    def exchange(lead, trail):
        top = pl.ds(pl.multiple_of(trail * share, 8), share)
        bottom = pl.ds(pl.multiple_of((orbitals + trail) * share, 8), share)
        real = products[lead, 0, top] + products[lead, 1, bottom]
        imaginary = products[lead, 1, top] - products[lead, 0, bottom]
        return real, imaginary

    def one_pair(holder, number):
        lead = pairs[holder, round_index, number, 0]
        trail = pairs[holder, round_index, number, 1]
        inverse = 1.0 / (energy_sum - (occupied[lead] + occupied[trail]))
        real, imaginary = exchange(lead, trail)
        swapped_real, swapped_imaginary = exchange(trail, lead)
        real, imaginary = real * inverse, imaginary * inverse
        return (
            2.0 * real - swapped_real * inverse,
            2.0 * imaginary - swapped_imaginary * inverse,
            real,
            imaginary,
        )

    def two_pairs(index, carry):
        low = one_pair(index, 0)
        high = one_pair(index, 1)
        c_re, c_im, a_re, a_im = (
            jnp.concatenate([x, y], axis=0).astype(jnp.bfloat16) for x, y in zip(low, high)
        )
        top = pl.ds(pl.multiple_of(index * 2 * share, 16), 2 * share)
        bottom = pl.ds(pl.multiple_of((count + index * 2) * share, 16), 2 * share)
        combined[top] = c_re
        combined[bottom] = c_im
        rounded[top] = a_re
        rounded[bottom] = a_im
        turned[top] = -a_im
        turned[bottom] = a_re
        return carry

    lax.fori_loop(0, devices, two_pairs, 0)
    contract_rows = (((0,), (0,)), ((), ()))
    for part, right in enumerate((rounded, turned)):
        total[part] = lax.dot_general(
            combined[...], right[...], contract_rows, preferred_element_type=jnp.float32
        )
    for place in range(LINE):
        for number, offset in enumerate((core, 1 - core)):
            cut = pl.ds(pl.multiple_of((place * CORES + offset) * share, 8), share)
            value = total[:, cut]
            if not earlier:
                outs[number][place] = value
                continue
            for local_index in range(2):
                added = jnp.where(mine == local_index, value, 0.0)
                for (term, which) in earlier:
                    added = added + jnp.where(which == local_index, term[number][place], 0.0)
                outs[number][place, local_index] = added


def piece_density(orders, held, conserve, pairs, here, occupied, own_energy, left, mates, before):
    momenta, orbitals, both, auxiliary = left.shape
    virtuals = both // 2
    share = virtuals // (LINE * CORES)
    count = pairs.shape[0] * pairs.shape[2]
    rows = 2 * orbitals * share
    leading = (LINE, momenta) if before else (LINE,)
    out_shape = (jax.ShapeDtypeStruct((*leading, 2, share, virtuals), jnp.float32),) * 2
    scalars = pl.BlockSpec(memory_space=pltpu.SMEM)
    whole = pl.BlockSpec(memory_space=pltpu.VMEM)
    return pl.pallas_call(
        functools.partial(piece_kernel, len(mates), len(before), orders, held),
        out_shape=out_shape,
        in_specs=[scalars] * 4
        + [whole] * (2 + len(mates) + len(before)),
        out_specs=(whole,) * len(out_shape),
        scratch_shapes=[
            pltpu.VMEM((rows + HEAD, auxiliary), jnp.bfloat16),
            pltpu.VMEM((orbitals, 2, rows, virtuals), jnp.float32),
            pltpu.VMEM((2 * count * share, virtuals), jnp.bfloat16),
            pltpu.VMEM((2 * count * share, virtuals), jnp.bfloat16),
            pltpu.VMEM((2 * count * share, virtuals), jnp.bfloat16),
            pltpu.VMEM((2, virtuals, virtuals), jnp.float32),
        ],
        compiler_params=pltpu.CompilerParams(vmem_limit_bytes=32 << 20),
        cost_estimate=pl.CostEstimate(
            flops=4 * rows * virtuals * auxiliary * orbitals + 8 * count * share * virtuals * virtuals,
            bytes_accessed=orbitals * both * auxiliary * 2 + 2 * rows * auxiliary,
            transcendentals=0,
        ),
    )(conserve, pairs, here, occupied, own_energy, left, *mates, *before)


def summed(keep, send):
    place = lax.axis_index("occ") // CORES
    devices = LINE * CORES
    held = keep + lax.ppermute(send, "occ", [(i, i ^ 1) for i in range(devices)])
    total = lax.dynamic_index_in_dim(held, place, 0, keepdims=False)
    for hop in range(1, LINE):
        part = lax.dynamic_index_in_dim(held, (place + hop) % LINE, 0, keepdims=False)
        ring = [(i, (i + CORES * hop) % devices) for i in range(devices)]
        total = total + lax.ppermute(part, "occ", ring)
    return total


def with_partner(array, reach):
    other = lax.ppermute(array, "occ", [(i, i ^ reach) for i in range(LINE * CORES)])
    return jnp.concatenate([array, other], axis=0)


def local(factors, occupied_energy, virtual_energy, conserve, pair_lists):
    momenta, orbitals, virtuals, _, auxiliary = factors.shape
    share = virtuals // (LINE * CORES)
    start = lax.axis_index("occ") * share
    column = lax.axis_index("ka") % COLUMNS
    here = jnp.stack([column, lax.axis_index("occ") % CORES]).astype(jnp.int32)

    def outgoing(momentum):
        cut = lax.dynamic_slice(
            factors, (momentum, 0, start, 0, 0), (1, orbitals, share, 2, auxiliary)
        )
        cut = jnp.transpose(cut[0], (2, 0, 1, 3)).reshape(2 * orbitals * share, auxiliary)
        energy = jnp.pad(virtual_energy[momentum : momentum + 1], ((0, 0), (0, auxiliary - virtuals)))
        first = jnp.broadcast_to(start.astype(jnp.bfloat16), (HEAD - 1, auxiliary))
        return jnp.concatenate([cut, energy, first], axis=0)

    pairs = with_partner(pair_lists[None], CORES)
    m0 = outgoing(0)
    m1 = outgoing(1)
    m0, m1, pairs, factors, here = lax.optimization_barrier((m0, m1, pairs, factors, here))
    plus = moved(m1, {0: (1, same), 1: (2, same), 2: (3, same), 3: (0, beside_next)})
    minus = moved(m1, {0: (3, same), 1: (0, same), 2: (1, beside_next), 3: (2, beside_next)})
    pairs = with_partner(with_partner(pairs, 2 * CORES), 1)
    m0, pairs, factors = lax.optimization_barrier((m0, pairs, factors))
    cross_one = moved(m0, {3: (0, onto_next)})
    own_energy = virtual_energy.astype(jnp.float32)[:, None, :]
    m0, plus, minus, factors, pairs, own_energy = lax.optimization_barrier(
        (m0, plus, minus, factors, pairs, own_energy)
    )
    two = moved(m0, {0: (2, same), 2: (0, onto_next)})
    up = moved(plus, {0: (0, across)})
    back = moved(minus, {0: (3, same), 1: (0, across), 2: (1, across), 3: (2, same)})
    near_one = moved(m0, {0: (1, same), 1: (2, same), 2: (3, same)})
    left = jnp.transpose(factors, (0, 1, 3, 2, 4)).reshape(momenta, orbitals, 2 * virtuals, auxiliary)
    m0, cross_one, left = lax.optimization_barrier((m0, cross_one, left))
    onward = moved(jnp.where(column == 0, cross_one, m0), {0: (1, same), 1: (3, same)})

    def density(orders, held, mates, before):
        return piece_density(
            orders, held, conserve, pairs, here, occupied_energy, own_energy, left, mates, before
        )

    orders = (((1, 0), (0, 1)), ((0,), (0,)), ((0, 1), (1, 0)), ((1,), (1,)))
    terms = density(orders[:1], (0, 1), (two, plus), ())
    *terms, cross_one, near_one = lax.optimization_barrier((*terms, cross_one, near_one))
    terms += density(orders[1:2], (0, 1), (cross_one, near_one), ())
    *terms, up, onward = lax.optimization_barrier((*terms, up, onward))
    terms += density(orders[2:3], (0, 1, 2, 1), (up, onward, two), ())
    total = density(orders, (0,), (back,), terms)
    return jnp.transpose(summed(*total), (0, 2, 1, 3))


def solution(mesh):
    in_specs = (
        P("ka", None, None, None, None),
        P(),
        P("ka", None),
        P("ka", None),
        P(None, "occ", None),
    )
    out_specs = P("ka", "occ", None, None)
    return jax.shard_map(local, mesh=mesh, in_specs=in_specs, out_specs=out_specs, check_vma=False)
```
